512 devices in a mesh: grp: 16 (over z_lo, x), sp: 32 (over z_hi, y, core).
Axes of the slice: x: 4, y: 8, z: 8 (z_hi: 2, z_lo: 4; z = z_hi * 4 + z_lo), core: 2. Of those that a mesh axis runs over, the one named last changes fastest.
Arguments:
- qkv: bfloat16 [16384, 3, 4096], P(('grp', 'sp')), may hold values from -128 to 128
- kv_cache: bfloat16 [32, 2, 3, 512, 4096], P('grp', None, None, None, 'sp'), may hold values from -6 to 6
- cycle_slot: int32 [32], P('grp'), may hold values from 0 to 2, as said below
- valid_count: int32 [32], P('grp'), may hold values from 0 to 3
- span_pos: int32 [32], P('grp'), may hold values from 0 to 63
- dec_in: bfloat16 [32, 3, 32, 32, 384], P('grp', None, 'sp'), may hold values from -6 to 6
- dec_cache: bfloat16 [32, 2, 32, 32, 384], P('sp', None, None, 'grp'), may hold values from -6 to 6
- time_weight: bfloat16 [3, 384, 768], replicated, may hold values from -0.1875 to 0.1875
- time_bias: float32 [768], replicated, may hold values from -3 to 3
Outputs:
- attention: bfloat16 [16384, 4096], P(('grp', 'sp'))
- decoded: bfloat16 [32, 6, 32, 32, 384], P('sp', None, None, 'grp')
The draws below stay inside these ranges and needn't reach their ends.
Inputs may be any that keep to these rules, and one draw needn't show every extreme that they name: Where valid_count is under 3, cycle_slot equals it.
All inputs are finite; a program needn't handle non-finite values.
Results may differ from the reference program's by a relative error of at most 0.03.
The reference program's roundings to bfloat16 on the way count: a program that leaves them out, or rounds other values in their place, can miss the bound.
Values may be sent and summed in bfloat16 or wider, within the bound.
A program may use at most 64 MiB of HBM per device.

```python
import math
import jax
import jax.numpy as jnp
from jax import lax

HS = 128
HEADS = 32
QW = 4096
VIDEOS = 32
VT = 512
CYCLE = 3
FRAMES = 3
CH = 384
BLOCKS = 32
BAND = 32


def draw_qkv(key, part):
    result = jnp.clip(jax.random.normal(key, (VIDEOS, VT, 3, HEADS, HS), jnp.float32), -6.0, 6.0)
    return result.reshape(VIDEOS * VT, 3, HEADS * HS).astype(jnp.bfloat16)


def cycle_state(key):
    base_key = jax.random.fold_in(key, 5)
    filled = jax.random.randint(jax.random.fold_in(base_key, 1), (VIDEOS,), 0, CYCLE + 1)
    chosen = jax.random.randint(jax.random.fold_in(base_key, 2), (), 0, VIDEOS)
    places = jnp.arange(VIDEOS, dtype=jnp.int32)
    filled = jnp.where(places == chosen, CYCLE, filled)
    replaced = jax.random.randint(jax.random.fold_in(base_key, 3), (VIDEOS,), 0, CYCLE)
    evicted = jnp.where(filled < CYCLE, filled, replaced)
    evicted = jnp.where(places == chosen, CYCLE - 1, evicted)
    return (evicted.astype(jnp.int32), filled.astype(jnp.int32))


def draw_cycle_slot(key, part):
    return cycle_state(key)[0]


def draw_valid_count(key, part):
    return cycle_state(key)[1]


def plant(values, key, low, top_value):
    longest = values.shape.index(max(values.shape))
    spots = []
    for shift in (0, 1):
        where = [jax.random.randint(jax.random.fold_in(key, axis), (), 0, length) for axis, length in enumerate(values.shape)]
        where[longest] = (where[longest] + shift) % values.shape[longest]
        spots.append(tuple(where))
    return values.at[spots[0]].set(low).at[spots[1]].set(top_value)


def levels(stream_key, extent, pieces, least, top_value):
    loudness, own = 1.0, jax.random.fold_in(stream_key, 6)
    for axis_at, parts in pieces:
        heights = jnp.exp(jax.random.uniform(jax.random.fold_in(own, axis_at), (parts,), jnp.float32, least / len(pieces), top_value / len(pieces)))
        loudness = loudness * jnp.repeat(heights, extent[axis_at] // parts).reshape([-1 if axis == axis_at else 1 for axis in range(len(extent))])
    return loudness


def gaussian(stream_key, shape, spread, bound, split=(), held_as=jnp.bfloat16):
    gain = levels(stream_key, shape, split, -0.22, 0.18) if split else 1.0
    values = jax.random.normal(stream_key, shape, jnp.float32) * spread * gain
    return jnp.minimum(jnp.maximum(values, -bound), bound).astype(held_as)


def setup_inputs(seed: int = 0) -> dict:
    splits = jax.random.split(jax.random.key(seed), 10)
    return {
        "qkv": draw_qkv(jax.random.fold_in(splits[9], 71), 0),
        "kv_cache": gaussian(splits[1], (VIDEOS, 2, CYCLE, VT, QW), 1.0, 6.0, ((0, 16), (4, 32))),
        "cycle_slot": draw_cycle_slot(jax.random.fold_in(splits[9], 71), 0),
        "valid_count": draw_valid_count(jax.random.fold_in(splits[9], 71), 0),
        "span_pos": plant(jax.random.randint(splits[4], (VIDEOS,), 0, 64), jax.random.fold_in(splits[4], 1), 0, 63).astype(jnp.int32),
        "dec_in": gaussian(splits[5], (VIDEOS, FRAMES, BLOCKS, BAND, CH), 1.0, 6.0, ((0, 16), (2, 32))),
        "dec_cache": gaussian(splits[6], (VIDEOS, 2, BLOCKS, BAND, CH), 1.0, 6.0, ((0, 32), (3, 16))),
        "time_weight": gaussian(splits[7], (3, CH, 2 * CH), (3 * CH) ** -0.5, 0.1875),
        "time_bias": gaussian(splits[8], (2 * CH,), 0.5, 3.0, (), jnp.float32),
    }


def rotate(values_in, span_start):
    half_dim = values_in.shape[-1] // 2
    frequency = jnp.exp(-math.log(10000.0) * jnp.arange(half_dim, dtype=jnp.float32) / half_dim)
    positions = (span_start * VT + jnp.arange(values_in.shape[0], dtype=jnp.int32)).astype(jnp.float32)
    angles = positions[:, None] * frequency[None, :]
    cosine = jnp.cos(angles)[:, None, :]
    sine_part = jnp.sin(angles)[:, None, :]
    first_half = values_in[..., :half_dim]
    second_half = values_in[..., half_dim:]
    return jnp.concatenate([first_half * cosine - second_half * sine_part, first_half * sine_part + second_half * cosine], -1)

def attend(inputs):
    tokens_block, cache_pair, evicted, filled, span_start = inputs
    queries = lax.optimization_barrier(rotate(tokens_block[:, 0].astype(jnp.float32), span_start).astype(jnp.bfloat16))
    key_now = lax.optimization_barrier(rotate(tokens_block[:, 1].astype(jnp.float32), span_start).astype(jnp.bfloat16))
    key_rows = jnp.concatenate([cache_pair[0].reshape(CYCLE * VT, HEADS, HS), key_now], 0)
    value_rows = jnp.concatenate([cache_pair[1].reshape(CYCLE * VT, HEADS, HS), tokens_block[:, 2]], 0)
    scores = jnp.einsum('thd,shd->hts', queries.astype(jnp.float32), key_rows.astype(jnp.float32)) / math.sqrt(HS)
    slot_index = jnp.arange((CYCLE + 1) * VT, dtype=jnp.int32) // VT
    valid_keys = (slot_index == CYCLE) | (slot_index < filled) & (slot_index != evicted)
    scores = jnp.where(valid_keys[None, None, :], scores, -jnp.inf)
    row_max = lax.optimization_barrier(jnp.max(scores, -1, keepdims=True))
    weights = jnp.exp(scores - row_max)
    weight_sum = lax.optimization_barrier(jnp.sum(weights, -1))
    rounded = lax.optimization_barrier(weights.astype(jnp.bfloat16))
    mixed_out = jnp.einsum('hts,shd->thd', rounded.astype(jnp.float32), value_rows.astype(jnp.float32))
    mixed_out = mixed_out / jnp.transpose(weight_sum)[:, :, None]
    return mixed_out.astype(jnp.bfloat16).reshape(VT, HEADS * HS)

def upsample_frames(latent, cached, time_weight, time_bias):
    shape_in = latent.shape
    frame_count = shape_in[1]
    channels = shape_in[-1]
    frames_all = jnp.concatenate([cached, latent], 1)
    conv_out = jnp.dot(frames_all[:, 0:frame_count].reshape(-1, channels), time_weight[0], preferred_element_type=jnp.float32)
    for offset in range(1, 3):
        conv_out = conv_out + jnp.dot(frames_all[:, offset:offset + frame_count].reshape(-1, channels), time_weight[offset], preferred_element_type=jnp.float32)
    conv_out = conv_out + time_bias.astype(jnp.float32)[None, :]
    conv_out = conv_out.reshape(shape_in[0], frame_count, shape_in[2], shape_in[3], 2, channels)
    conv_out = jnp.moveaxis(conv_out, 4, 2)
    return conv_out.reshape(shape_in[0], 2 * frame_count, shape_in[2], shape_in[3], channels).astype(jnp.bfloat16)

def reference(qkv, kv_cache, cycle_slot, valid_count, span_pos, dec_in, dec_cache, time_weight, time_bias):
    blocks_all = qkv.reshape(VIDEOS, VT, 3, HEADS, HS)
    caches_all = kv_cache.reshape(VIDEOS, 2, CYCLE, VT, HEADS, HS)
    mixed_all = lax.map(attend, (blocks_all, caches_all, cycle_slot, valid_count, span_pos))
    attention = mixed_all.reshape(VIDEOS * VT, HEADS * HS)

    def decode_one(pair_in):
        return upsample_frames(pair_in[0][None], pair_in[1][None], time_weight, time_bias)[0]
    decoded = lax.map(decode_one, (dec_in, dec_cache))
    return (attention, decoded)
```

```python
import math

import jax
import jax.numpy as jnp
import numpy as np
from jax import lax
from jax.experimental import pallas as pl
from jax.experimental.pallas import tpu as pltpu
from jax.sharding import PartitionSpec as P

HS = 128
CYCLE = 3
MESH = pl.DeviceIdType.MESH
NEG = -1e30
C2 = math.log2(math.e) / math.sqrt(HS)
HALF = 16
TOK = 32
VT = 512
FR = 3
CH = 384
LT = CH // 128


def rope_tables():
    f = np.exp(-math.log(10000.0) * np.arange(64, dtype=np.float64) / 64)
    ang = np.arange(VT, dtype=np.float64)[:, None] * np.concatenate([f, f])[None, :]
    sign = np.concatenate([-np.ones(64), np.ones(64)])
    return np.cos(ang).astype(np.float32), (np.sin(ang) * sign).astype(np.float32)


def dot_t(a, b):
    return lax.dot_general(a, b, (((1,), (1,)), ((), ())), preferred_element_type=jnp.float32)


def dot(a, b):
    return lax.dot_general(a, b, (((1,), (0,)), ((), ())), preferred_element_type=jnp.float32)


def attend(q, parts):
    scores = [dot_t(q, k) if bias is None else dot_t(q, k) + bias for k, _, bias in parts]
    top = jnp.max(scores[0], axis=1, keepdims=True)
    for s in scores[1:]:
        top = jnp.maximum(top, jnp.max(s, axis=1, keepdims=True))
    top = top * C2
    total, acc = None, None
    for s, (_, v, _) in zip(scores, parts):
        w = jnp.exp2(s * C2 - top)
        t = jnp.sum(w, axis=1, keepdims=True)
        o = dot(w.astype(jnp.bfloat16), v)
        total = t if total is None else total + t
        acc = o if acc is None else acc + o
    return top, total, acc


def kernel(
    slot_ref, count_ref, base_ref, qkv, cache_hbm, dec_in, dec_cache, weight_hbm, bias_ref, cos_hbm, sin_hbm,
    out, decoded,
    rx, fq, oc, oc_out, lse_in, lse_out, ob, cache, weight, tabs, cosv, sinv, kself, sendd, frames, outd,
    s_send, s_fwd, s_oc, s_o, s_dec, r_qb, r_a, r_b, r_fq, r_oc, r_lse, r_o, r_dec, l_own, l_cache, l_w, l_tab, l_dc, l_ds, l_out,
):
    g = lax.axis_index("grp")
    s = lax.axis_index("sp")
    half = s // HALF
    me = s % HALF
    y = me // 2
    c = me % 2
    partner = (s + HALF) % 32
    other = 1 - half

    def peer(k, cc):
        step = (k // 2 + 1) * (1 - 2 * (k % 2))
        return ((y + step + 8) % 8) * 2 + (c + cc) % 2

    def for_peers(fn):
        def body(i, _):
            fn(peer(i // 2, i % 2))
            return 0
        lax.fori_loop(0, 14, body, 0)
        fn(y * 2 + (1 - c))

    bar = pltpu.get_barrier_semaphore()
    for_peers(lambda t: pl.semaphore_signal(bar, 1, device_id=(g, half * HALF + t), device_id_type=MESH))
    pl.semaphore_signal(bar, 1, device_id=(g, partner), device_id_type=MESH)
    src_g = s // 2
    mine = (src_g == g).astype(jnp.int32)

    def greet(i, _):
        pl.semaphore_signal(bar, 1, device_id=(src_g, (s + 1 + i) % 32), device_id_type=MESH)
        return 0
    lax.fori_loop(0, 31, greet, 0)

    @pl.when(src_g != g)
    def _():
        pl.semaphore_signal(bar, 1, device_id=(src_g, s), device_id_type=MESH)

    def cols(h):
        return pl.ds(pl.multiple_of(h * HS, HS), HS)

    head = (s, partner)
    own = [pltpu.make_async_copy(qkv.at[:, :, cols(head[j])], rx.at[j, :, me], l_own.at[j]) for j in range(2)]
    for cp in own:
        cp.start()
    c_tab = [pltpu.make_async_copy(h, tabs.at[i], l_tab.at[i]) for i, h in enumerate((cos_hbm, sin_hbm))]
    for cp in c_tab:
        cp.start()
    c_ds = pltpu.make_async_copy
    ds_copies = []
    for v in range(2):
        for j in range(LT):
            cp = pltpu.make_async_copy(dec_in.at[v, :, 0, :, pl.ds(j * 128, 128)], sendd.reshape(2, FR, LT, 32, 128).at[v, :, j], l_ds.at[v * LT + j])
            cp.start()
            ds_copies.append(cp)
    c_cache = pltpu.make_async_copy(cache_hbm, cache, l_cache)
    c_cache.start()
    dc_copies = []
    for j in range(LT):
        cp = pltpu.make_async_copy(dec_cache.at[0, :, :, :, pl.ds(j * 128, 128)], frames.at[pl.ds(0, 2), j], l_dc.at[j])
        cp.start()
        dc_copies.append(cp)
    c_w = pltpu.make_async_copy(weight_hbm, weight, l_w)
    c_w.start()

    pl.semaphore_wait(bar, 15 + 1 + 32 - mine)

    def send(part, n, j, t, rsem):
        pltpu.make_async_remote_copy(
            qkv.at[pl.ds(part, n), :, cols(half * HALF + t if j == 0 else other * HALF + t)],
            rx.at[j, pl.ds(part, n), me], s_send, rsem,
            device_id=(g, half * HALF + t), device_id_type=MESH,
        ).start()

    for_peers(lambda t: send(0, 1, 1, t, r_qb.at[me]))
    for_peers(lambda t: send(0, 3, 0, t, r_a))
    for cp in ds_copies:
        cp.wait()

    def send_frames(gd, v):
        return pltpu.make_async_remote_copy(
            sendd.at[v, :, :, gd], frames.at[pl.ds(2, FR), :, s], s_dec, r_dec,
            device_id=(gd, 2 * g + v), device_id_type=MESH,
        )

    def send_far(i, _):
        send_frames((g + 1 + i // 2) % 16, i % 2).start()
        return 0
    lax.fori_loop(0, 30, send_far, 0)
    for v in range(2):
        @pl.when(s != 2 * g + v)
        def _():
            send_frames(g, v).start()

        @pl.when(s == 2 * g + v)
        def _():
            pltpu.make_async_copy(sendd.at[v, :, :, g], frames.at[pl.ds(2, FR), :, s], r_dec).start()
    for_peers(lambda t: send(1, 2, 1, t, r_b))

    for cp in c_tab:
        cp.wait()

    def make_tables(i, _):
        rows = pl.ds(pl.multiple_of(i * 128, 128), 128)
        ct, st = tabs[0, rows, :], tabs[1, rows, :]
        for v in range(2):
            cb, sb = base_ref[pl.ds(v, 1), :], base_ref[pl.ds(2 + v, 1), :]
            cosv[v, rows, :] = ct * cb - st * sb
            sinv[v, rows, :] = st * cb + ct * sb
        return 0
    lax.fori_loop(0, 4, make_tables, 0)

    def rotate(x, v, row, n):
        x = x.astype(jnp.float32)
        rows = pl.ds(pl.multiple_of(row, n), n)
        return (x * cosv[v, rows, :] + pltpu.roll(x, 64, 1) * sinv[v, rows, :]).astype(jnp.bfloat16)

    def forward(t):
        pltpu.make_async_remote_copy(
            rx.at[1, 0, t], fq.at[t], s_fwd, r_fq.at[t // 4],
            device_id=(g, partner), device_id_type=MESH,
        ).start()

    for cp in own:
        cp.wait()
    forward(me)

    def wait_forward(t):
        pltpu.make_async_copy(rx.at[1, 0, t], rx.at[1, 0, t], r_qb.at[t]).wait()
        forward(t)
    for_peers(wait_forward)

    eye = lax.broadcasted_iota(jnp.int32, (128, 128), 0) == lax.broadcasted_iota(jnp.int32, (128, 128), 1)

    def slots(v):
        cs, vc = slot_ref[v], count_ref[v]
        s0 = jnp.where(cs == 0, 1, 0)
        s1 = jnp.where(cs == 2, 1, 2)
        return [(sl, jnp.where(sl < vc, 0.0, NEG)) for sl in (s0, s1)]

    c_cache.wait()
    there = slots(other)

    def cross(i, _):
        pltpu.make_async_copy(fq.at[pl.ds(i * 4, 4)], fq.at[pl.ds(i * 4, 4)], r_fq.at[i]).wait()
        q = rotate(fq[pl.ds(i * 4, 4)].reshape(128, HS), other, i * 128, 128)
        top, total, acc = attend(q, [(cache[other, 0, sl], cache[other, 1, sl], b) for sl, b in there])
        oc_out[i] = (acc / total).astype(jnp.bfloat16)
        lse = jnp.broadcast_to(top + jnp.log2(total), (128, 128))
        lse_out[i] = jnp.broadcast_to(jnp.sum(jnp.where(eye, lse, 0.0), axis=0, keepdims=True), (8, 128))
        pltpu.make_async_remote_copy(oc_out.at[i], oc.at[i], s_oc.at[0], r_oc.at[i], device_id=(g, partner), device_id_type=MESH).start()
        pltpu.make_async_remote_copy(lse_out.at[i], lse_in.at[i], s_oc.at[1], r_lse.at[i], device_id=(g, partner), device_id_type=MESH).start()
        return 0
    lax.fori_loop(0, 4, cross, 0)

    def send_out(j, t):
        pltpu.make_async_remote_copy(
            ob.at[j, t], out.at[:, cols(head[j])], s_o, r_o,
            device_id=(g, half * HALF + t), device_id_type=MESH,
        ).start()

    def own_out(j):
        return pltpu.make_async_copy(ob.at[j, me], out.at[:, cols(head[j])], l_own.at[j])

    def rotate_keys(j):
        def body(i, _):
            kself[pl.ds(pl.multiple_of(i * 128, 128), 128), :] = rotate(rx[j, 1, pl.ds(i * 4, 4)].reshape(128, HS), half, i * 128, 128)
            return 0
        lax.fori_loop(0, 4, body, 0)

    pltpu.make_async_copy(rx.at[0, :, pl.ds(0, 15)], rx.at[0, :, pl.ds(0, 15)], r_a).wait()
    here = slots(half)
    rotate_keys(0)

    def whole(i, _):
        q = rotate(rx[0, 0, pl.ds(i * 8, 8)].reshape(256, HS), half, i * 256, 256)
        parts = [(cache[half, 0, sl], cache[half, 1, sl], b) for sl, b in here]
        parts.append((kself[...], rx[0, 2].reshape(VT, HS), None))
        top, total, acc = attend(q, parts)
        ob[0, pl.ds(i * 8, 8)] = (acc / total).astype(jnp.bfloat16).reshape(8, TOK, HS)
        return 0
    lax.fori_loop(0, 2, whole, 0)
    for_peers(lambda t: send_out(0, t))
    own_out(0).start()

    for cp in dc_copies:
        cp.wait()
    c_w.wait()
    pltpu.make_async_copy(frames.at[pl.ds(2, FR)], frames.at[pl.ds(2, FR)], r_dec).wait()
    fview = frames.reshape(5, LT, 64, 128)
    oview = outd.reshape(6, LT, 64, 128)
    lhs = [jnp.concatenate([fview[pl.ds(tap, FR), j].reshape(FR * 64, 128) for j in range(LT)], axis=1) for tap in range(3)]
    for i in range(2):
        n = pl.ds(i * CH, CH)
        conv = dot(lhs[0], weight[0, :, n]) + dot(lhs[1], weight[1, :, n]) + dot(lhs[2], weight[2, :, n])
        conv = (conv + bias_ref[:, n]).astype(jnp.bfloat16)
        for t in range(FR):
            for j in range(LT):
                oview[2 * t + i, j] = conv[t * 64:(t + 1) * 64, j * 128:(j + 1) * 128]
    o_copies = []
    for j in range(LT):
        cp = pltpu.make_async_copy(outd.at[:, j], decoded.at[0, :, :, :, pl.ds(j * 128, 128)], l_out.at[j])
        cp.start()
        o_copies.append(cp)

    pltpu.make_async_copy(rx.at[1, pl.ds(1, 2), pl.ds(0, 15)], rx.at[1, pl.ds(1, 2), pl.ds(0, 15)], r_b).wait()
    rotate_keys(1)

    def merged(i, _):
        q = rotate(rx[1, 0, pl.ds(i * 4, 4)].reshape(128, HS), half, i * 128, 128)
        top, total, acc = attend(q, [(kself[...], rx[1, 2].reshape(VT, HS), None)])
        pltpu.make_async_copy(lse_in.at[i], lse_in.at[i], r_lse.at[i]).wait()
        pltpu.make_async_copy(oc.at[i], oc.at[i], r_oc.at[i]).wait()
        lse = jnp.broadcast_to(lse_in[i, 0:1, :], (128, 128))
        lse = jnp.sum(jnp.where(eye, lse, 0.0), axis=1, keepdims=True)
        both = jnp.maximum(lse, top)
        wc = jnp.exp2(lse - both)
        ws = jnp.exp2(top - both)
        mixed = (oc[i].astype(jnp.float32) * wc + acc * ws) / (wc + total * ws)
        ob[1, pl.ds(i * 4, 4)] = mixed.astype(jnp.bfloat16).reshape(4, TOK, HS)
        return 0
    lax.fori_loop(0, 4, merged, 0)
    for_peers(lambda t: send_out(1, t))
    own_out(1).start()

    own_out(0).wait()
    own_out(1).wait()
    for cp in o_copies:
        cp.wait()
    piece = rx.at[:, :, pl.ds(0, 15)]
    pltpu.make_async_copy(piece, piece, s_send).wait()
    pltpu.make_async_copy(fq, fq, s_fwd).wait()
    pltpu.make_async_copy(oc, oc, s_oc.at[0]).wait()
    pltpu.make_async_copy(lse_in, lse_in, s_oc.at[1]).wait()
    piece = rx.at[:, 0, pl.ds(0, 15)]
    pltpu.make_async_copy(piece, piece, s_o).wait()

    @pl.when(s // 2 != g)
    def _():
        pltpu.make_async_copy(frames.at[pl.ds(2, FR)], frames.at[pl.ds(2, FR)], s_dec).wait()

    @pl.when(s // 2 == g)
    def _():
        part = frames.at[pl.ds(2, FR), :, pl.ds(0, 31)]
        pltpu.make_async_copy(part, part, s_dec).wait()
    pltpu.make_async_copy(piece, piece, r_o).wait()


def on_device(qkv, kv_cache, cycle_slot, valid_count, span_pos, dec_in, dec_cache, time_weight, time_bias):
    f = np.exp(-math.log(10000.0) * np.arange(64, dtype=np.float64) / 64)
    freq = jnp.asarray(np.concatenate([f, f]).astype(np.float32))
    sign = jnp.asarray(np.concatenate([-np.ones(64), np.ones(64)]).astype(np.float32))
    ang = (span_pos * VT).astype(jnp.float32)[:, None] * freq[None, :]
    base = jnp.concatenate([jnp.cos(ang), jnp.sin(ang) * sign[None, :]], 0)
    cos_t, sin_t = rope_tables()
    bf, f32 = jnp.bfloat16, jnp.float32
    vmem, hbm, smem = pltpu.VMEM, pl.BlockSpec(memory_space=pl.ANY), pl.BlockSpec(memory_space=pltpu.SMEM)
    inv = pl.BlockSpec(memory_space=pltpu.VMEM)
    dma = pltpu.SemaphoreType.DMA
    return pl.pallas_call(
        kernel,
        out_shape=(
            jax.ShapeDtypeStruct((TOK, 32 * HS), bf),
            jax.ShapeDtypeStruct((1, 2 * FR, 32, 2, CH), bf),
        ),
        in_specs=[smem, smem, inv, hbm, hbm, hbm, hbm, hbm, inv, hbm, hbm],
        out_specs=(hbm, hbm),
        scratch_shapes=[
            vmem((2, 3, HALF, TOK, HS), bf),
            vmem((HALF, TOK, HS), bf),
            vmem((4, 128, HS), bf),
            vmem((4, 128, HS), bf),
            vmem((4, 8, 128), f32),
            vmem((4, 8, 128), f32),
            vmem((2, HALF, TOK, HS), bf),
            vmem((2, 2, CYCLE, VT, HS), bf),
            vmem((3, CH, 2 * CH), bf),
            vmem((2, VT, HS), f32),
            vmem((2, VT, HS), f32),
            vmem((2, VT, HS), f32),
            vmem((VT, HS), bf),
            vmem((2, FR, LT, 16, 2, 128), bf),
            vmem((5, LT, 32, 2, 128), bf),
            vmem((6, LT, 32, 2, 128), bf),
            dma, dma, dma((2,)), dma, dma,
            dma((HALF,)), dma, dma, dma((4,)), dma((4,)), dma((4,)), dma, dma,
            dma((2,)), dma, dma, dma((2,)), dma((LT,)), dma((2 * LT,)), dma((LT,)),
        ],
        name="rollout",
        compiler_params=pltpu.CompilerParams(collective_id=0, has_side_effects=True, vmem_limit_bytes=48 * 1024 * 1024),
    )(
        cycle_slot, valid_count, base, jnp.transpose(qkv, (1, 0, 2)), kv_cache, dec_in, dec_cache,
        time_weight, time_bias.reshape(1, 2 * CH), jnp.asarray(cos_t), jnp.asarray(sin_t),
    )


def solution(mesh):
    placed = (
        P(("grp", "sp"), None, None),
        P("grp", None, None, None, "sp"),
        P("grp"),
        P("grp"),
        P("grp"),
        P("grp", None, "sp", None, None),
        P("sp", None, None, "grp", None),
        P(),
        P(),
    )
    return jax.shard_map(
        on_device,
        mesh=mesh,
        in_specs=placed,
        out_specs=(P(("grp", "sp"), None), P("sp", None, None, "grp", None)),
        check_vma=False,
    )
```

```python
import math

import jax
import jax.numpy as jnp
import numpy as np
from jax import lax
from jax.experimental import pallas as pl
from jax.experimental.pallas import tpu as pltpu
from jax.sharding import PartitionSpec as P

HS = 128
CYCLE = 3
MESH = pl.DeviceIdType.MESH
NEG = -1e30
C2 = math.log2(math.e) / math.sqrt(HS)
HALF = 16
TOK = 32
VT = 512
SPANS = 64
FR = 3
CH = 384
LT = CH // 128


def rope_tables():
    f = np.exp(-math.log(10000.0) * np.arange(64, dtype=np.float64) / 64)
    steps = np.concatenate([np.arange(VT), VT * np.arange(SPANS)]).astype(np.float64)
    ang = steps[:, None] * np.concatenate([f, f])[None, :]
    sign = np.concatenate([-np.ones(64), np.ones(64)])
    return np.stack([np.cos(ang), np.sin(ang) * sign]).astype(np.float32)


def dot_t(a, b):
    return lax.dot_general(a, b, (((1,), (1,)), ((), ())), preferred_element_type=jnp.float32)


def dot(a, b):
    return lax.dot_general(a, b, (((1,), (0,)), ((), ())), preferred_element_type=jnp.float32)


def attend(q, parts):
    scores = [dot_t(q, k) if bias is None else dot_t(q, k) + bias for k, _, bias in parts]
    top = jnp.max(scores[0], axis=1, keepdims=True)
    for s in scores[1:]:
        top = jnp.maximum(top, jnp.max(s, axis=1, keepdims=True))
    top = top * C2
    total, acc = None, None
    for s, (_, v, _) in zip(scores, parts):
        w = jnp.exp2(s * C2 - top)
        t = jnp.sum(w, axis=1, keepdims=True)
        o = dot(w.astype(jnp.bfloat16), v)
        total = t if total is None else total + t
        acc = o if acc is None else acc + o
    return top, total, acc


def kernel(
    slot_ref, count_ref, pos_ref, qkv, cache_hbm, dec_in, dec_cache, weight_hbm, bias_hbm, tab_hbm,
    out, decoded,
    rx, fq, oc, oc_out, lse_in, lse_out, ob, cache, weight, bias_ref, tabs, cosv, sinv, kself, sendd, mid, frames, outd,
    s_send, s_fwd, s_oc, s_o, s_dec, r_qb, r_a, r_b, r_fq, r_oc, r_lse, r_o, r_dec, r_mid, l_own, l_cache, l_w, l_bias, l_tab, l_dc, l_ds, l_out,
):
    g = lax.axis_index("grp")
    s = lax.axis_index("sp")
    half = s // HALF
    me = s % HALF
    y = me // 2
    c = me % 2
    partner = (s + HALF) % 32
    other = 1 - half

    def peer(k, cc):
        step = jnp.where(k == 0, 4, ((8 - k) // 2) * (1 - 2 * (k % 2)))
        return ((y + step + 8) % 8) * 2 + (c + cc) % 2

    def for_peers(fn):
        def body(i, _):
            fn(peer(i // 2, i % 2))
            return 0
        lax.fori_loop(0, 14, body, 0)
        fn(y * 2 + (1 - c))

    bar = pltpu.get_barrier_semaphore()
    for_peers(lambda t: pl.semaphore_signal(bar, 1, device_id=(g, half * HALF + t), device_id_type=MESH))
    pl.semaphore_signal(bar, 1, device_id=(g, partner), device_id_type=MESH)
    def near_half(i):
        return half * 8 + i // 2, (i % 2) * HALF + me

    def greet(i, _):
        gs, ss = near_half((i + 2 * g) % 16)

        @pl.when(jnp.logical_not((gs == g) & (ss == s)))
        def _():
            pl.semaphore_signal(bar, 1, device_id=(gs, ss), device_id_type=MESH)
        return 0
    lax.fori_loop(0, 16, greet, 0)
    mine = (g // 8 == half).astype(jnp.int32)

    def cols(h):
        return pl.ds(pl.multiple_of(h * HS, HS), HS)

    head = (s, partner)
    own = [pltpu.make_async_copy(qkv.at[:, :, cols(head[j])], rx.at[j, :, me], l_own.at[j]) for j in range(2)]
    for cp in own:
        cp.start()
    c_tab = pltpu.make_async_copy(tab_hbm, tabs, l_tab)
    c_tab.start()
    ds_copies = []
    for v in range(2):
        for j in range(LT):
            cp = pltpu.make_async_copy(dec_in.at[v, :, 0, :, pl.ds(j * 128, 128)], sendd.reshape(2, FR, LT, 32, 128).at[v, :, j], l_ds.at[v * LT + j])
            cp.start()
            ds_copies.append(cp)
    c_cache = pltpu.make_async_copy(cache_hbm, cache, l_cache)
    c_cache.start()
    dc_copies = []
    for j in range(LT):
        cp = pltpu.make_async_copy(dec_cache.at[0, :, :, :, pl.ds(j * 128, 128)], frames.reshape(5, LT, 32, 2, 128).at[pl.ds(0, 2), j], l_dc.at[j])
        cp.start()
        dc_copies.append(cp)
    c_w = pltpu.make_async_copy(weight_hbm, weight, l_w)
    c_w.start()
    c_b = pltpu.make_async_copy(bias_hbm, bias_ref, l_bias)
    c_b.start()

    pl.semaphore_wait(bar, 15 + 1 + 16 - mine)

    def send(part, n, j, t, rsem):
        pltpu.make_async_remote_copy(
            qkv.at[pl.ds(part, n), :, cols(half * HALF + t if j == 0 else other * HALF + t)],
            rx.at[j, pl.ds(part, n), me], s_send, rsem,
            device_id=(g, half * HALF + t), device_id_type=MESH,
        ).start()

    for cp in ds_copies:
        cp.wait()

    def send_stage(i, _):
        gd, sd = (g + i) % 16, (g // 8) * HALF + me
        src, dst = sendd.at[:, :, :, gd], mid.at[g % 8, :, :, :, half]
        itself = (gd == g) & (sd == s)

        @pl.when(jnp.logical_not(itself))
        def _():
            pltpu.make_async_remote_copy(src, dst, s_dec.at[0], r_mid, device_id=(gd, sd), device_id_type=MESH).start()

        @pl.when(itself)
        def _():
            pltpu.make_async_copy(src, dst, r_mid).start()
        return 0

    lax.fori_loop(0, 16, send_stage, 0)
    for_peers(lambda t: send(0, 1, 1, t, r_qb.at[me]))
    for_peers(lambda t: send(0, 3, 0, t, r_a))
    for_peers(lambda t: send(1, 2, 1, t, r_b))

    c_tab.wait()
    bases = [[tabs[i, pl.ds(VT + pos_ref[v], 1), :] for i in range(2)] for v in range(2)]

    def make_tables(i, _):
        rows = pl.ds(pl.multiple_of(i * 128, 128), 128)
        ct, st = tabs[0, rows, :], tabs[1, rows, :]
        for v in range(2):
            cb, sb = bases[v]
            cosv[v, rows, :] = ct * cb - st * sb
            sinv[v, rows, :] = st * cb + ct * sb
        return 0
    lax.fori_loop(0, 4, make_tables, 0)

    def rotate(x, v, row, n):
        x = x.astype(jnp.float32)
        rows = pl.ds(pl.multiple_of(row, n), n)
        return (x * cosv[v, rows, :] + pltpu.roll(x, 64, 1) * sinv[v, rows, :]).astype(jnp.bfloat16)

    def forward(t):
        pltpu.make_async_remote_copy(
            rx.at[1, 0, t], fq.at[t], s_fwd, r_fq.at[t // 4],
            device_id=(g, partner), device_id_type=MESH,
        ).start()

    for cp in own:
        cp.wait()
    forward(me)

    def wait_forward(t):
        pltpu.make_async_copy(rx.at[1, 0, t], rx.at[1, 0, t], r_qb.at[t]).wait()
        forward(t)
    for_peers(wait_forward)

    pltpu.make_async_copy(mid, mid, r_mid).wait()
    fresh = frames.at[pl.ds(2, FR)]

    def send_frames(t):
        pltpu.make_async_remote_copy(
            mid.at[t // 2, t % 2], fresh.at[:, :, :, me], s_dec.at[1], r_dec,
            device_id=(g, half * HALF + t), device_id_type=MESH,
        ).start()
    for_peers(send_frames)
    pltpu.make_async_copy(mid.at[me // 2, me % 2], fresh.at[:, :, :, me], r_dec).start()

    eye = lax.broadcasted_iota(jnp.int32, (128, 128), 0) == lax.broadcasted_iota(jnp.int32, (128, 128), 1)

    def slots(v):
        cs, vc = slot_ref[v], count_ref[v]
        s0 = jnp.where(cs == 0, 1, 0)
        s1 = jnp.where(cs == 2, 1, 2)
        return [(sl, jnp.where(sl < vc, 0.0, NEG)) for sl in (s0, s1)]

    c_cache.wait()
    there = slots(other)

    def cross(i, _):
        pltpu.make_async_copy(fq.at[pl.ds(i * 4, 4)], fq.at[pl.ds(i * 4, 4)], r_fq.at[i]).wait()
        q = rotate(fq[pl.ds(i * 4, 4)].reshape(128, HS), other, i * 128, 128)
        top, total, acc = attend(q, [(cache[other, 0, sl], cache[other, 1, sl], b) for sl, b in there])
        oc_out[i] = (acc / total).astype(jnp.bfloat16)
        lse = jnp.broadcast_to(top + jnp.log2(total), (128, 128))
        lse_out[i] = jnp.broadcast_to(jnp.sum(jnp.where(eye, lse, 0.0), axis=0, keepdims=True), (8, 128))
        pltpu.make_async_remote_copy(oc_out.at[i], oc.at[i], s_oc.at[0], r_oc.at[i], device_id=(g, partner), device_id_type=MESH).start()
        pltpu.make_async_remote_copy(lse_out.at[i], lse_in.at[i], s_oc.at[1], r_lse.at[i], device_id=(g, partner), device_id_type=MESH).start()
        return 0
    lax.fori_loop(0, 4, cross, 0)

    def send_out(j, t):
        pltpu.make_async_remote_copy(
            ob.at[j, t], out.at[:, cols(head[j])], s_o, r_o,
            device_id=(g, half * HALF + t), device_id_type=MESH,
        ).start()

    def own_out(j):
        return pltpu.make_async_copy(ob.at[j, me], out.at[:, cols(head[j])], l_own.at[j])

    def rotate_keys(j):
        def body(i, _):
            kself[pl.ds(pl.multiple_of(i * 128, 128), 128), :] = rotate(rx[j, 1, pl.ds(i * 4, 4)].reshape(128, HS), half, i * 128, 128)
            return 0
        lax.fori_loop(0, 4, body, 0)

    pltpu.make_async_copy(rx.at[0, :, pl.ds(0, 15)], rx.at[0, :, pl.ds(0, 15)], r_a).wait()
    here = slots(half)
    rotate_keys(0)

    def whole(i, _):
        q = rotate(rx[0, 0, pl.ds(i * 8, 8)].reshape(256, HS), half, i * 256, 256)
        parts = [(cache[half, 0, sl], cache[half, 1, sl], b) for sl, b in here]
        parts.append((kself[...], rx[0, 2].reshape(VT, HS), None))
        top, total, acc = attend(q, parts)
        ob[0, pl.ds(i * 8, 8)] = (acc / total).astype(jnp.bfloat16).reshape(8, TOK, HS)
        return 0
    lax.fori_loop(0, 2, whole, 0)
    for_peers(lambda t: send_out(0, t))
    own_out(0).start()

    for cp in dc_copies:
        cp.wait()
    c_w.wait()
    c_b.wait()
    pltpu.make_async_copy(fresh, fresh, r_dec).wait()
    fview = frames.reshape(5, LT, 64, 128)
    oview = outd.reshape(6, LT, 64, 128)
    lhs = [jnp.concatenate([fview[pl.ds(tap, FR), j].reshape(FR * 64, 128) for j in range(LT)], axis=1) for tap in range(3)]
    for i in range(2):
        n = pl.ds(i * CH, CH)
        conv = dot(lhs[0], weight[0, :, n]) + dot(lhs[1], weight[1, :, n]) + dot(lhs[2], weight[2, :, n])
        conv = (conv + bias_ref[n].reshape(1, CH)).astype(jnp.bfloat16)
        for t in range(FR):
            for j in range(LT):
                oview[2 * t + i, j] = conv[t * 64:(t + 1) * 64, j * 128:(j + 1) * 128]
    o_copies = []
    for j in range(LT):
        cp = pltpu.make_async_copy(outd.at[:, j], decoded.at[0, :, :, :, pl.ds(j * 128, 128)], l_out.at[j])
        cp.start()
        o_copies.append(cp)

    pltpu.make_async_copy(rx.at[1, pl.ds(1, 2), pl.ds(0, 15)], rx.at[1, pl.ds(1, 2), pl.ds(0, 15)], r_b).wait()
    rotate_keys(1)

    def merged(i, _):
        q = rotate(rx[1, 0, pl.ds(i * 4, 4)].reshape(128, HS), half, i * 128, 128)
        top, total, acc = attend(q, [(kself[...], rx[1, 2].reshape(VT, HS), None)])
        pltpu.make_async_copy(lse_in.at[i], lse_in.at[i], r_lse.at[i]).wait()
        pltpu.make_async_copy(oc.at[i], oc.at[i], r_oc.at[i]).wait()
        lse = jnp.broadcast_to(lse_in[i, 0:1, :], (128, 128))
        lse = jnp.sum(jnp.where(eye, lse, 0.0), axis=1, keepdims=True)
        both = jnp.maximum(lse, top)
        wc = jnp.exp2(lse - both)
        ws = jnp.exp2(top - both)
        mixed = (oc[i].astype(jnp.float32) * wc + acc * ws) / (wc + total * ws)
        ob[1, pl.ds(i * 4, 4)] = mixed.astype(jnp.bfloat16).reshape(4, TOK, HS)
        return 0
    lax.fori_loop(0, 4, merged, 0)
    for_peers(lambda t: send_out(1, t))
    own_out(1).start()

    own_out(0).wait()
    own_out(1).wait()
    for cp in o_copies:
        cp.wait()
    piece = rx.at[:, :, pl.ds(0, 15)]
    pltpu.make_async_copy(piece, piece, s_send).wait()
    pltpu.make_async_copy(fq, fq, s_fwd).wait()
    pltpu.make_async_copy(oc, oc, s_oc.at[0]).wait()
    pltpu.make_async_copy(lse_in, lse_in, s_oc.at[1]).wait()
    piece = rx.at[:, 0, pl.ds(0, 15)]
    pltpu.make_async_copy(piece, piece, s_o).wait()

    part = frames.at[pl.ds(2, FR), :, :, pl.ds(0, 15)]
    pltpu.make_async_copy(part, part, s_dec.at[1]).wait()

    @pl.when(g // 8 != half)
    def _():
        pltpu.make_async_copy(sendd, sendd, s_dec.at[0]).wait()

    @pl.when(g // 8 == half)
    def _():
        part = sendd.at[:, :, :, pl.ds(0, 15)]
        pltpu.make_async_copy(part, part, s_dec.at[0]).wait()
    pltpu.make_async_copy(piece, piece, r_o).wait()


def on_device(qkv, kv_cache, cycle_slot, valid_count, span_pos, dec_in, dec_cache, time_weight, time_bias):
    bf, f32 = jnp.bfloat16, jnp.float32
    vmem, hbm, smem = pltpu.VMEM, pl.BlockSpec(memory_space=pl.ANY), pl.BlockSpec(memory_space=pltpu.SMEM)
    dma = pltpu.SemaphoreType.DMA
    return pl.pallas_call(
        kernel,
        out_shape=(
            jax.ShapeDtypeStruct((TOK, 32 * HS), bf),
            jax.ShapeDtypeStruct((1, 2 * FR, 32, 2, CH), bf),
        ),
        in_specs=[smem, smem, smem] + [hbm] * 7,
        out_specs=(hbm, hbm),
        scratch_shapes=[
            vmem((2, 3, HALF, TOK, HS), bf),
            vmem((HALF, TOK, HS), bf),
            vmem((4, 128, HS), bf),
            vmem((4, 128, HS), bf),
            vmem((4, 8, 128), f32),
            vmem((4, 8, 128), f32),
            vmem((2, HALF, TOK, HS), bf),
            vmem((2, 2, CYCLE, VT, HS), bf),
            vmem((3, CH, 2 * CH), bf),
            vmem((2 * CH,), f32),
            vmem((2, VT + SPANS, HS), f32),
            vmem((2, VT, HS), f32),
            vmem((2, VT, HS), f32),
            vmem((VT, HS), bf),
            vmem((2, FR, LT, 16, 2, 128), bf),
            vmem((8, 2, FR, LT, 2, 2, 128), bf),
            vmem((5, LT, 2, 16, 2, 128), bf),
            vmem((6, LT, 32, 2, 128), bf),
            dma, dma, dma((2,)), dma, dma((2,)),
            dma((HALF,)), dma, dma, dma((4,)), dma((4,)), dma((4,)), dma, dma, dma,
            dma((2,)), dma, dma, dma, dma, dma((LT,)), dma((2 * LT,)), dma((LT,)),
        ],
        name="rollout",
        compiler_params=pltpu.CompilerParams(collective_id=0, has_side_effects=True, vmem_limit_bytes=67043328),
    )(
        cycle_slot, valid_count, span_pos, jnp.transpose(qkv, (1, 0, 2)), kv_cache, dec_in, dec_cache,
        time_weight, time_bias, jnp.asarray(rope_tables()),
    )


def solution(mesh):
    placed = (
        P(("grp", "sp"), None, None),
        P("grp", None, None, None, "sp"),
        P("grp"),
        P("grp"),
        P("grp"),
        P("grp", None, "sp", None, None),
        P("sp", None, None, "grp", None),
        P(),
        P(),
    )
    return jax.shard_map(
        on_device,
        mesh=mesh,
        in_specs=placed,
        out_specs=(P(("grp", "sp"), None), P("sp", None, None, "grp", None)),
        check_vma=False,
    )
```

```python
import math

import jax
import jax.numpy as jnp
import numpy as np
from jax import lax
from jax.experimental import pallas as pl
from jax.experimental.pallas import tpu as pltpu
from jax.sharding import PartitionSpec as P

HS = 128
CYCLE = 3
MESH = pl.DeviceIdType.MESH
NEG = -1e30
C2 = math.log2(math.e) / math.sqrt(HS)
HALF = 16
TOK = 32
VT = 512
SPANS = 64
FR = 3
CH = 384
LT = CH // 128


def rope_tables():
    f = np.exp(-math.log(10000.0) * np.arange(64, dtype=np.float64) / 64)
    steps = np.concatenate([np.arange(VT), VT * np.arange(SPANS)]).astype(np.float64)
    ang = steps[:, None] * np.concatenate([f, f])[None, :]
    sign = np.concatenate([-np.ones(64), np.ones(64)])
    return np.stack([np.cos(ang), np.sin(ang) * sign]).astype(np.float32)


def dot_t(a, b):
    return lax.dot_general(a, b, (((1,), (1,)), ((), ())), preferred_element_type=jnp.float32)


def dot(a, b):
    return lax.dot_general(a, b, (((1,), (0,)), ((), ())), preferred_element_type=jnp.float32)


def attend(q, parts):
    scores = [dot_t(q, k) if bias is None else dot_t(q, k) + bias for k, _, bias in parts]
    top = jnp.max(scores[0], axis=1, keepdims=True)
    for s in scores[1:]:
        top = jnp.maximum(top, jnp.max(s, axis=1, keepdims=True))
    top = top * C2
    total, acc = None, None
    for s, (_, v, _) in zip(scores, parts):
        w = jnp.exp2(s * C2 - top)
        t = jnp.sum(w, axis=1, keepdims=True)
        o = dot(w.astype(jnp.bfloat16), v)
        total = t if total is None else total + t
        acc = o if acc is None else acc + o
    return top, total, acc


def kernel(
    slot_hbm, count_hbm, pos_hbm, qkv, cache_hbm, dec_in, dec_cache, weight_hbm, bias_hbm, tab_hbm,
    out, decoded,
    slot_ref, count_ref, pos_ref, rx, fq, oc, oc_out, lse_in, lse_out, ob, cache, weight, bias_ref, tabs, cosv, sinv, kself, sendd, mid, frames, outd,
    s_send, s_fwd, s_oc, s_o, s_dec, r_qb, r_a, r_b, r_fq, r_oc, r_lse, r_o, r_dec, r_mid, l_state, l_own, l_cache, l_w, l_bias, l_tab, l_dc, l_ds, l_out,
):
    g = lax.axis_index("grp")
    s = lax.axis_index("sp")
    half = s // HALF
    me = s % HALF
    y = me // 2
    c = me % 2
    partner = (s + HALF) % 32
    other = 1 - half

    def peer(k, cc):
        step = jnp.where(k == 0, 4, ((8 - k) // 2) * (1 - 2 * (k % 2)))
        return ((y + step + 8) % 8) * 2 + (c + cc) % 2

    def for_peers(fn):
        def body(i, _):
            fn(peer(i // 2, i % 2))
            return 0
        lax.fori_loop(0, 14, body, 0)
        fn(y * 2 + (1 - c))

    bar = pltpu.get_barrier_semaphore()
    for_peers(lambda t: pl.semaphore_signal(bar, 1, device_id=(g, half * HALF + t), device_id_type=MESH))
    pl.semaphore_signal(bar, 1, device_id=(g, partner), device_id_type=MESH)
    def near_half(i):
        return half * 8 + i // 2, (i % 2) * HALF + me

    def greet(i, _):
        gs, ss = near_half((i + 2 * g) % 16)

        @pl.when(jnp.logical_not((gs == g) & (ss == s)))
        def _():
            pl.semaphore_signal(bar, 1, device_id=(gs, ss), device_id_type=MESH)
        return 0
    lax.fori_loop(0, 16, greet, 0)
    mine = (g // 8 == half).astype(jnp.int32)

    def cols(h):
        return pl.ds(pl.multiple_of(h * HS, HS), HS)

    head = (s, partner)
    own = [pltpu.make_async_copy(qkv.at[:, :, cols(head[j])], rx.at[j, :, me], l_own.at[j]) for j in range(2)]
    for cp in own:
        cp.start()
    c_state = [
        pltpu.make_async_copy(h, r, l_state.at[i])
        for i, (h, r) in enumerate(((slot_hbm, slot_ref), (count_hbm, count_ref), (pos_hbm, pos_ref)))
    ]
    for cp in c_state:
        cp.start()
    c_tab = pltpu.make_async_copy(tab_hbm, tabs, l_tab)
    c_tab.start()
    ds_copies = []
    for v in range(2):
        for j in range(LT):
            cp = pltpu.make_async_copy(dec_in.at[v, :, 0, :, pl.ds(j * 128, 128)], sendd.reshape(2, FR, LT, 32, 128).at[v, :, j], l_ds.at[v * LT + j])
            cp.start()
            ds_copies.append(cp)
    c_cache = pltpu.make_async_copy(cache_hbm, cache, l_cache)
    c_cache.start()
    dc_copies = []
    for j in range(LT):
        cp = pltpu.make_async_copy(dec_cache.at[0, :, :, :, pl.ds(j * 128, 128)], frames.reshape(5, LT, 32, 2, 128).at[pl.ds(0, 2), j], l_dc.at[j])
        cp.start()
        dc_copies.append(cp)
    c_w = pltpu.make_async_copy(weight_hbm, weight, l_w)
    c_w.start()
    c_b = pltpu.make_async_copy(bias_hbm, bias_ref, l_bias)
    c_b.start()

    pl.semaphore_wait(bar, 15 + 1 + 16 - mine)

    def send(part, n, j, t, rsem):
        pltpu.make_async_remote_copy(
            qkv.at[pl.ds(part, n), :, cols(half * HALF + t if j == 0 else other * HALF + t)],
            rx.at[j, pl.ds(part, n), me], s_send, rsem,
            device_id=(g, half * HALF + t), device_id_type=MESH,
        ).start()

    for cp in ds_copies:
        cp.wait()

    def send_stage(i, _):
        gd, sd = (g + i) % 16, (g // 8) * HALF + me
        src, dst = sendd.at[:, :, :, gd], mid.at[g % 8, :, :, :, half]
        itself = (gd == g) & (sd == s)

        @pl.when(jnp.logical_not(itself))
        def _():
            pltpu.make_async_remote_copy(src, dst, s_dec.at[0], r_mid, device_id=(gd, sd), device_id_type=MESH).start()

        @pl.when(itself)
        def _():
            pltpu.make_async_copy(src, dst, r_mid).start()
        return 0

    lax.fori_loop(0, 16, send_stage, 0)
    for_peers(lambda t: send(0, 1, 1, t, r_qb.at[me]))
    for_peers(lambda t: send(0, 3, 0, t, r_a))
    for_peers(lambda t: send(1, 2, 1, t, r_b))

    c_tab.wait()
    for cp in c_state:
        cp.wait()
    bases = [[tabs[i, pl.ds(VT + pos_ref[v], 1), :] for i in range(2)] for v in range(2)]

    def make_tables(i, _):
        rows = pl.ds(pl.multiple_of(i * 128, 128), 128)
        ct, st = tabs[0, rows, :], tabs[1, rows, :]
        for v in range(2):
            cb, sb = bases[v]
            cosv[v, rows, :] = ct * cb - st * sb
            sinv[v, rows, :] = st * cb + ct * sb
        return 0
    lax.fori_loop(0, 4, make_tables, 0)

    def rotate(x, v, row, n):
        x = x.astype(jnp.float32)
        rows = pl.ds(pl.multiple_of(row, n), n)
        return (x * cosv[v, rows, :] + pltpu.roll(x, 64, 1) * sinv[v, rows, :]).astype(jnp.bfloat16)

    def forward(t):
        pltpu.make_async_remote_copy(
            rx.at[1, 0, t], fq.at[t], s_fwd, r_fq.at[t // 4],
            device_id=(g, partner), device_id_type=MESH,
        ).start()

    for cp in own:
        cp.wait()
    forward(me)

    def wait_forward(t):
        pltpu.make_async_copy(rx.at[1, 0, t], rx.at[1, 0, t], r_qb.at[t]).wait()
        forward(t)
    for_peers(wait_forward)

    pltpu.make_async_copy(mid, mid, r_mid).wait()
    fresh = frames.at[pl.ds(2, FR)]

    def send_frames(t):
        pltpu.make_async_remote_copy(
            mid.at[t // 2, t % 2], fresh.at[:, :, :, me], s_dec.at[1], r_dec,
            device_id=(g, half * HALF + t), device_id_type=MESH,
        ).start()
    for_peers(send_frames)
    pltpu.make_async_copy(mid.at[me // 2, me % 2], fresh.at[:, :, :, me], r_dec).start()

    eye = lax.broadcasted_iota(jnp.int32, (128, 128), 0) == lax.broadcasted_iota(jnp.int32, (128, 128), 1)

    def slots(v):
        cs, vc = slot_ref[v], count_ref[v]
        s0 = jnp.where(cs == 0, 1, 0)
        s1 = jnp.where(cs == 2, 1, 2)
        return [(sl, jnp.where(sl < vc, 0.0, NEG)) for sl in (s0, s1)]

    c_cache.wait()
    there = slots(other)

    def cross(i, _):
        pltpu.make_async_copy(fq.at[pl.ds(i * 4, 4)], fq.at[pl.ds(i * 4, 4)], r_fq.at[i]).wait()
        q = rotate(fq[pl.ds(i * 4, 4)].reshape(128, HS), other, i * 128, 128)
        top, total, acc = attend(q, [(cache[other, 0, sl], cache[other, 1, sl], b) for sl, b in there])
        oc_out[i] = (acc / total).astype(jnp.bfloat16)
        lse = jnp.broadcast_to(top + jnp.log2(total), (128, 128))
        lse_out[i] = jnp.broadcast_to(jnp.sum(jnp.where(eye, lse, 0.0), axis=0, keepdims=True), (8, 128))
        pltpu.make_async_remote_copy(oc_out.at[i], oc.at[i], s_oc.at[0], r_oc.at[i], device_id=(g, partner), device_id_type=MESH).start()
        pltpu.make_async_remote_copy(lse_out.at[i], lse_in.at[i], s_oc.at[1], r_lse.at[i], device_id=(g, partner), device_id_type=MESH).start()
        return 0
    lax.fori_loop(0, 4, cross, 0)

    def send_out(j, t):
        pltpu.make_async_remote_copy(
            ob.at[j, t], out.at[:, cols(head[j])], s_o, r_o,
            device_id=(g, half * HALF + t), device_id_type=MESH,
        ).start()

    def own_out(j):
        return pltpu.make_async_copy(ob.at[j, me], out.at[:, cols(head[j])], l_own.at[j])

    def rotate_keys(j):
        def body(i, _):
            kself[pl.ds(pl.multiple_of(i * 128, 128), 128), :] = rotate(rx[j, 1, pl.ds(i * 4, 4)].reshape(128, HS), half, i * 128, 128)
            return 0
        lax.fori_loop(0, 4, body, 0)

    pltpu.make_async_copy(rx.at[0, :, pl.ds(0, 15)], rx.at[0, :, pl.ds(0, 15)], r_a).wait()
    here = slots(half)
    rotate_keys(0)

    def whole(i, _):
        q = rotate(rx[0, 0, pl.ds(i * 8, 8)].reshape(256, HS), half, i * 256, 256)
        parts = [(cache[half, 0, sl], cache[half, 1, sl], b) for sl, b in here]
        parts.append((kself[...], rx[0, 2].reshape(VT, HS), None))
        top, total, acc = attend(q, parts)
        ob[0, pl.ds(i * 8, 8)] = (acc / total).astype(jnp.bfloat16).reshape(8, TOK, HS)
        return 0
    lax.fori_loop(0, 2, whole, 0)
    for_peers(lambda t: send_out(0, t))
    own_out(0).start()

    pltpu.make_async_copy(rx.at[1, pl.ds(1, 2), pl.ds(0, 15)], rx.at[1, pl.ds(1, 2), pl.ds(0, 15)], r_b).wait()
    rotate_keys(1)

    def merged(i, _):
        q = rotate(rx[1, 0, pl.ds(i * 4, 4)].reshape(128, HS), half, i * 128, 128)
        top, total, acc = attend(q, [(kself[...], rx[1, 2].reshape(VT, HS), None)])
        pltpu.make_async_copy(lse_in.at[i], lse_in.at[i], r_lse.at[i]).wait()
        pltpu.make_async_copy(oc.at[i], oc.at[i], r_oc.at[i]).wait()
        lse = jnp.broadcast_to(lse_in[i, 0:1, :], (128, 128))
        lse = jnp.sum(jnp.where(eye, lse, 0.0), axis=1, keepdims=True)
        both = jnp.maximum(lse, top)
        wc = jnp.exp2(lse - both)
        ws = jnp.exp2(top - both)
        mixed = (oc[i].astype(jnp.float32) * wc + acc * ws) / (wc + total * ws)
        ob[1, pl.ds(i * 4, 4)] = mixed.astype(jnp.bfloat16).reshape(4, TOK, HS)
        return 0
    lax.fori_loop(0, 4, merged, 0)
    for_peers(lambda t: send_out(1, t))
    own_out(1).start()

    for cp in dc_copies:
        cp.wait()
    c_w.wait()
    c_b.wait()
    pltpu.make_async_copy(fresh, fresh, r_dec).wait()
    fview = frames.reshape(5, LT, 64, 128)
    oview = outd.reshape(6, LT, 64, 128)
    lhs = [jnp.concatenate([fview[pl.ds(tap, FR), j].reshape(FR * 64, 128) for j in range(LT)], axis=1) for tap in range(3)]
    for i in range(2):
        n = pl.ds(i * CH, CH)
        conv = dot(lhs[0], weight[0, :, n]) + dot(lhs[1], weight[1, :, n]) + dot(lhs[2], weight[2, :, n])
        conv = (conv + bias_ref[n].reshape(1, CH)).astype(jnp.bfloat16)
        for t in range(FR):
            for j in range(LT):
                oview[2 * t + i, j] = conv[t * 64:(t + 1) * 64, j * 128:(j + 1) * 128]
    o_copies = []
    for j in range(LT):
        cp = pltpu.make_async_copy(outd.at[:, j], decoded.at[0, :, :, :, pl.ds(j * 128, 128)], l_out.at[j])
        cp.start()
        o_copies.append(cp)

    own_out(0).wait()
    own_out(1).wait()
    for cp in o_copies:
        cp.wait()
    piece = rx.at[:, :, pl.ds(0, 15)]
    pltpu.make_async_copy(piece, piece, s_send).wait()
    pltpu.make_async_copy(fq, fq, s_fwd).wait()
    pltpu.make_async_copy(oc, oc, s_oc.at[0]).wait()
    pltpu.make_async_copy(lse_in, lse_in, s_oc.at[1]).wait()
    piece = rx.at[:, 0, pl.ds(0, 15)]
    pltpu.make_async_copy(piece, piece, s_o).wait()

    part = frames.at[pl.ds(2, FR), :, :, pl.ds(0, 15)]
    pltpu.make_async_copy(part, part, s_dec.at[1]).wait()

    @pl.when(g // 8 != half)
    def _():
        pltpu.make_async_copy(sendd, sendd, s_dec.at[0]).wait()

    @pl.when(g // 8 == half)
    def _():
        part = sendd.at[:, :, :, pl.ds(0, 15)]
        pltpu.make_async_copy(part, part, s_dec.at[0]).wait()
    pltpu.make_async_copy(piece, piece, r_o).wait()


def put_out(a, b, a_out, b_out, sem):
    copies = [pltpu.make_async_copy(x, o, sem.at[i]) for i, (x, o) in enumerate(((a, a_out), (b, b_out)))]
    for cp in copies:
        cp.start()
    for cp in copies:
        cp.wait()


def on_device(qkv, kv_cache, cycle_slot, valid_count, span_pos, dec_in, dec_cache, time_weight, time_bias):
    bf, f32 = jnp.bfloat16, jnp.float32
    hbm, free = pl.BlockSpec(memory_space=pltpu.MemorySpace.HBM), pl.BlockSpec(memory_space=pl.ANY)
    vmem, smem = pltpu.VMEM, pltpu.SMEM
    dma = pltpu.SemaphoreType.DMA
    operands = (
        cycle_slot, valid_count, span_pos, jnp.transpose(qkv, (1, 0, 2)), kv_cache, dec_in, dec_cache,
        time_weight, time_bias, jnp.asarray(rope_tables()),
    )
    shapes = (
        jax.ShapeDtypeStruct((TOK, 32 * HS), bf),
        jax.ShapeDtypeStruct((1, 2 * FR, 32, 2, CH), bf),
    )
    results = pl.pallas_call(
        kernel,
        out_shape=shapes,
        in_specs=[hbm] * 10,
        out_specs=(free, free),
        scratch_shapes=[
            smem((2,), jnp.int32), smem((2,), jnp.int32), smem((2,), jnp.int32),
            vmem((2, 3, HALF, TOK, HS), bf),
            vmem((HALF, TOK, HS), bf),
            vmem((4, 128, HS), bf),
            vmem((4, 128, HS), bf),
            vmem((4, 8, 128), f32),
            vmem((4, 8, 128), f32),
            vmem((2, HALF, TOK, HS), bf),
            vmem((2, 2, CYCLE, VT, HS), bf),
            vmem((3, CH, 2 * CH), bf),
            vmem((2 * CH,), f32),
            vmem((2, VT + SPANS, HS), f32),
            vmem((2, VT, HS), f32),
            vmem((2, VT, HS), f32),
            vmem((VT, HS), bf),
            vmem((2, FR, LT, 16, 2, 128), bf),
            vmem((8, 2, FR, LT, 2, 2, 128), bf),
            vmem((5, LT, 2, 16, 2, 128), bf),
            vmem((6, LT, 32, 2, 128), bf),
            dma, dma, dma((2,)), dma, dma((2,)),
            dma((HALF,)), dma, dma, dma((4,)), dma((4,)), dma((4,)), dma, dma, dma,
            dma((3,)), dma((2,)), dma, dma, dma, dma, dma((LT,)), dma((2 * LT,)), dma((LT,)),
        ],
        name="rollout",
        compiler_params=pltpu.CompilerParams(collective_id=0, has_side_effects=True, vmem_limit_bytes=20 * 1024 * 1024),
    )(
        *(pltpu.with_memory_space_constraint(x, pltpu.MemorySpace.HBM) for x in operands)
    )
    return pl.pallas_call(
        put_out,
        out_shape=shapes,
        in_specs=[free, free],
        out_specs=(hbm, hbm),
        scratch_shapes=[dma((2,))],
        name="put_out",
        compiler_params=pltpu.CompilerParams(vmem_limit_bytes=1024 * 1024),
    )(*results)


def solution(mesh):
    placed = (
        P(("grp", "sp"), None, None),
        P("grp", None, None, None, "sp"),
        P("grp"),
        P("grp"),
        P("grp"),
        P("grp", None, "sp", None, None),
        P("sp", None, None, "grp", None),
        P(),
        P(),
    )
    return jax.shard_map(
        on_device,
        mesh=mesh,
        in_specs=placed,
        out_specs=(P(("grp", "sp"), None), P("sp", None, None, "grp", None)),
        check_vma=False,
    )
```

```python
import math

import jax
import jax.numpy as jnp
import numpy as np
from jax import lax
from jax.experimental import pallas as pl
from jax.experimental.pallas import tpu as pltpu
from jax.sharding import PartitionSpec as P

HS = 128
CYCLE = 3
MESH = pl.DeviceIdType.MESH
NEG = -1e30
C2 = math.log2(math.e) / math.sqrt(HS)
HALF = 16
TOK = 32
VT = 512
SPANS = 64
FR = 3
CH = 384
LT = CH // 128


def rope_tables():
    f = np.exp(-math.log(10000.0) * np.arange(64, dtype=np.float64) / 64)
    steps = np.concatenate([np.arange(VT), VT * np.arange(SPANS)]).astype(np.float64)
    ang = steps[:, None] * np.concatenate([f, f])[None, :]
    sign = np.concatenate([-np.ones(64), np.ones(64)])
    return np.stack([np.cos(ang), np.sin(ang) * sign]).astype(np.float32)


def dot_t(a, b):
    return lax.dot_general(a, b, (((1,), (1,)), ((), ())), preferred_element_type=jnp.float32)


def dot(a, b):
    return lax.dot_general(a, b, (((1,), (0,)), ((), ())), preferred_element_type=jnp.float32)


def attend(q, parts):
    scores = [dot_t(q, k) if bias is None else dot_t(q, k) + bias for k, _, bias in parts]
    top = jnp.max(scores[0], axis=1, keepdims=True)
    for s in scores[1:]:
        top = jnp.maximum(top, jnp.max(s, axis=1, keepdims=True))
    top = top * C2
    total, acc = None, None
    for s, (_, v, _) in zip(scores, parts):
        w = jnp.exp2(s * C2 - top)
        t = jnp.sum(w, axis=1, keepdims=True)
        o = dot(w.astype(jnp.bfloat16), v)
        total = t if total is None else total + t
        acc = o if acc is None else acc + o
    return top, total, acc


def kernel(
    slot_hbm, count_hbm, pos_hbm, qkv, cache_hbm, dec_in, dec_cache, weight_hbm, bias_hbm, tab_hbm,
    out, decoded,
    slot_ref, count_ref, pos_ref, rx, fq, oc, oc_out, lse_in, lse_out, ob, cache, weight, bias_ref, tabs, cosv, sinv, kself, sendd, mid, frames, outd,
    s_send, s_fwd, s_oc, s_o, s_dec, r_qb, r_a, r_b, r_fq, r_oc, r_lse, r_o, r_dec, r_mid, l_state, l_own, l_cache, l_w, l_bias, l_tab, l_dc, l_ds, l_out,
):
    g = lax.axis_index("grp")
    s = lax.axis_index("sp")
    half = s // HALF
    me = s % HALF
    y = me // 2
    c = me % 2
    partner = (s + HALF) % 32
    other = 1 - half

    def peer(k, cc):
        step = jnp.where(k == 0, 4, ((8 - k) // 2) * (1 - 2 * (k % 2)))
        return ((y + step + 8) % 8) * 2 + (c + cc) % 2

    def for_peers(fn):
        def body(i, _):
            fn(peer(i // 2, i % 2))
            return 0
        lax.fori_loop(0, 14, body, 0)
        fn(y * 2 + (1 - c))

    bar = pltpu.get_barrier_semaphore()
    for_peers(lambda t: pl.semaphore_signal(bar, 1, device_id=(g, half * HALF + t), device_id_type=MESH))
    def greet(i, _):
        pl.semaphore_signal(bar, 1, device_id=((g + 1 + i) % 16, s), device_id_type=MESH)
        return 0

    @pl.when(half == 1)
    def _():
        lax.fori_loop(0, 15, greet, 0)

    def cols(h):
        return pl.ds(pl.multiple_of(h * HS, HS), HS)

    head = (s, partner)
    own = [pltpu.make_async_copy(qkv.at[:, :, cols(head[j])], rx.at[j, :, me], l_own.at[j]) for j in range(2)]
    for cp in own:
        cp.start()
    c_state = [
        pltpu.make_async_copy(h, r, l_state.at[i])
        for i, (h, r) in enumerate(((slot_hbm, slot_ref), (count_hbm, count_ref), (pos_hbm, pos_ref)))
    ]
    for cp in c_state:
        cp.start()
    c_tab = pltpu.make_async_copy(tab_hbm, tabs, l_tab)
    c_tab.start()
    ds_copies = []
    for v in range(2):
        for j in range(LT):
            cp = pltpu.make_async_copy(dec_in.at[v, :, 0, :, pl.ds(j * 128, 128)], sendd.reshape(2, FR, LT, 32, 128).at[v, :, j], l_ds.at[v * LT + j])
            cp.start()
            ds_copies.append(cp)
    c_cache = pltpu.make_async_copy(cache_hbm, cache, l_cache)
    c_cache.start()
    dc_copies = []
    for j in range(LT):
        cp = pltpu.make_async_copy(dec_cache.at[0, :, :, :, pl.ds(j * 128, 128)], frames.reshape(5, LT, 32, 2, 128).at[pl.ds(0, 2), j], l_dc.at[j])
        cp.start()
        dc_copies.append(cp)
    c_w = pltpu.make_async_copy(weight_hbm, weight, l_w)
    c_w.start()
    c_b = pltpu.make_async_copy(bias_hbm, bias_ref, l_bias)
    c_b.start()

    pl.semaphore_wait(bar, 15 + 31 * half)

    def report(i, _):
        pl.semaphore_signal(bar, 1, device_id=((g + i) % 16, partner), device_id_type=MESH)
        return 0

    @pl.when(half == 0)
    def _():
        lax.fori_loop(0, 16, report, 0)

    @pl.when(half == 1)
    def _():
        pl.semaphore_signal(bar, 1, device_id=(g, partner), device_id_type=MESH)

    def send(part, n, j, t, rsem):
        pltpu.make_async_remote_copy(
            qkv.at[pl.ds(part, n), :, cols(half * HALF + t if j == 0 else other * HALF + t)],
            rx.at[j, pl.ds(part, n), me], s_send, rsem,
            device_id=(g, half * HALF + t), device_id_type=MESH,
        ).start()

    for_peers(lambda t: send(0, 1, 1, t, r_qb.at[me]))
    for_peers(lambda t: send(0, 3, 0, t, r_a))
    for_peers(lambda t: send(1, 2, 1, t, r_b))

    c_tab.wait()
    for cp in c_state:
        cp.wait()
    bases = [[tabs[i, pl.ds(VT + pos_ref[v], 1), :] for i in range(2)] for v in range(2)]

    def make_tables(i, _):
        rows = pl.ds(pl.multiple_of(i * 128, 128), 128)
        ct, st = tabs[0, rows, :], tabs[1, rows, :]
        for v in range(2):
            cb, sb = bases[v]
            cosv[v, rows, :] = ct * cb - st * sb
            sinv[v, rows, :] = st * cb + ct * sb
        return 0
    lax.fori_loop(0, 4, make_tables, 0)

    def rotate(x, v, row, n):
        x = x.astype(jnp.float32)
        rows = pl.ds(pl.multiple_of(row, n), n)
        return (x * cosv[v, rows, :] + pltpu.roll(x, 64, 1) * sinv[v, rows, :]).astype(jnp.bfloat16)

    @pl.when(half == 0)
    def _():
        pl.semaphore_wait(bar, 1)

    for cp in ds_copies:
        cp.wait()

    def send_stage(i, _):
        gd, sd = (g + i) % 16, (g // 8) * HALF + me
        src, dst = sendd.at[:, :, :, gd], mid.at[g % 8, :, :, :, half]
        itself = (gd == g) & (sd == s)

        @pl.when(jnp.logical_not(itself))
        def _():
            pltpu.make_async_remote_copy(src, dst, s_dec.at[0], r_mid, device_id=(gd, sd), device_id_type=MESH).start()

        @pl.when(itself)
        def _():
            pltpu.make_async_copy(src, dst, r_mid).start()
        return 0

    lax.fori_loop(0, 16, send_stage, 0)

    def forward(t):
        pltpu.make_async_remote_copy(
            rx.at[1, 0, t], fq.at[t], s_fwd, r_fq.at[t // 4],
            device_id=(g, partner), device_id_type=MESH,
        ).start()

    for cp in own:
        cp.wait()
    forward(me)

    def wait_forward(t):
        pltpu.make_async_copy(rx.at[1, 0, t], rx.at[1, 0, t], r_qb.at[t]).wait()
        forward(t)
    for_peers(wait_forward)

    eye = lax.broadcasted_iota(jnp.int32, (128, 128), 0) == lax.broadcasted_iota(jnp.int32, (128, 128), 1)

    def slots(v):
        cs, vc = slot_ref[v], count_ref[v]
        s0 = jnp.where(cs == 0, 1, 0)
        s1 = jnp.where(cs == 2, 1, 2)
        return [(sl, jnp.where(sl < vc, 0.0, NEG)) for sl in (s0, s1)]

    def send_out(j, t):
        pltpu.make_async_remote_copy(
            ob.at[j, t], out.at[:, cols(head[j])], s_o, r_o,
            device_id=(g, half * HALF + t), device_id_type=MESH,
        ).start()

    def own_out(j):
        return pltpu.make_async_copy(ob.at[j, me], out.at[:, cols(head[j])], l_own.at[j])

    def rotate_keys(j):
        def body(i, _):
            kself[pl.ds(pl.multiple_of(i * 128, 128), 128), :] = rotate(rx[j, 1, pl.ds(i * 4, 4)].reshape(128, HS), half, i * 128, 128)
            return 0
        lax.fori_loop(0, 4, body, 0)

    def far_chunk(k):
        return (k + y // 2 + 2) % 4

    def serve_partner():
        there = slots(other)

        def cross(k, _):
            i = far_chunk(k)
            pltpu.make_async_copy(fq.at[pl.ds(i * 4, 4)], fq.at[pl.ds(i * 4, 4)], r_fq.at[i]).wait()
            q = rotate(fq[pl.ds(i * 4, 4)].reshape(128, HS), other, i * 128, 128)
            top, total, acc = attend(q, [(cache[other, 0, sl], cache[other, 1, sl], b) for sl, b in there])
            oc_out[i] = (acc / total).astype(jnp.bfloat16)
            lse = jnp.broadcast_to(top + jnp.log2(total), (128, 128))
            lse_out[i] = jnp.broadcast_to(jnp.sum(jnp.where(eye, lse, 0.0), axis=0, keepdims=True), (8, 128))
            pltpu.make_async_remote_copy(oc_out.at[i], oc.at[i], s_oc.at[0], r_oc.at[i], device_id=(g, partner), device_id_type=MESH).start()
            pltpu.make_async_remote_copy(lse_out.at[i], lse_in.at[i], s_oc.at[1], r_lse.at[i], device_id=(g, partner), device_id_type=MESH).start()
            return 0
        lax.fori_loop(0, 4, cross, 0)

    def own_head():
        pltpu.make_async_copy(rx.at[0, :, pl.ds(0, 15)], rx.at[0, :, pl.ds(0, 15)], r_a).wait()
        here = slots(half)
        rotate_keys(0)

        def whole(i, _):
            q = rotate(rx[0, 0, pl.ds(i * 8, 8)].reshape(256, HS), half, i * 256, 256)
            parts = [(cache[half, 0, sl], cache[half, 1, sl], b) for sl, b in here]
            parts.append((kself[...], rx[0, 2].reshape(VT, HS), None))
            top, total, acc = attend(q, parts)
            ob[0, pl.ds(i * 8, 8)] = (acc / total).astype(jnp.bfloat16).reshape(8, TOK, HS)
            return 0
        lax.fori_loop(0, 2, whole, 0)
        for_peers(lambda t: send_out(0, t))
        own_out(0).start()

    c_cache.wait()

    @pl.when(half == 1)
    def _():
        serve_partner()

    @pl.when(half == 0)
    def _():
        own_head()

    @pl.when(half == 1)
    def _():
        own_head()

    @pl.when(half == 0)
    def _():
        serve_partner()

    pltpu.make_async_copy(mid, mid, r_mid).wait()
    fresh = frames.at[pl.ds(2, FR)]

    def send_frames(t):
        pltpu.make_async_remote_copy(
            mid.at[t // 2, t % 2], fresh.at[:, :, :, me], s_dec.at[1], r_dec,
            device_id=(g, half * HALF + t), device_id_type=MESH,
        ).start()
    for_peers(send_frames)
    pltpu.make_async_copy(mid.at[me // 2, me % 2], fresh.at[:, :, :, me], r_dec).start()

    pltpu.make_async_copy(rx.at[1, pl.ds(1, 2), pl.ds(0, 15)], rx.at[1, pl.ds(1, 2), pl.ds(0, 15)], r_b).wait()
    rotate_keys(1)

    def merged(k, _):
        i = far_chunk(k)
        q = rotate(rx[1, 0, pl.ds(i * 4, 4)].reshape(128, HS), half, i * 128, 128)
        top, total, acc = attend(q, [(kself[...], rx[1, 2].reshape(VT, HS), None)])
        pltpu.make_async_copy(lse_in.at[i], lse_in.at[i], r_lse.at[i]).wait()
        pltpu.make_async_copy(oc.at[i], oc.at[i], r_oc.at[i]).wait()
        lse = jnp.broadcast_to(lse_in[i, 0:1, :], (128, 128))
        lse = jnp.sum(jnp.where(eye, lse, 0.0), axis=1, keepdims=True)
        both = jnp.maximum(lse, top)
        wc = jnp.exp2(lse - both)
        ws = jnp.exp2(top - both)
        mixed = (oc[i].astype(jnp.float32) * wc + acc * ws) / (wc + total * ws)
        ob[1, pl.ds(i * 4, 4)] = mixed.astype(jnp.bfloat16).reshape(4, TOK, HS)

        def hand_out(b, _):
            t = i * 4 + b

            @pl.when(t != me)
            def _():
                send_out(1, t)

            @pl.when(t == me)
            def _():
                own_out(1).start()
            return 0
        lax.fori_loop(0, 4, hand_out, 0)
        return 0
    lax.fori_loop(0, 4, merged, 0)

    for cp in dc_copies:
        cp.wait()
    c_w.wait()
    c_b.wait()
    pltpu.make_async_copy(fresh, fresh, r_dec).wait()
    fview = frames.reshape(5, LT, 64, 128)
    oview = outd.reshape(6, LT, 64, 128)
    lhs = [jnp.concatenate([fview[pl.ds(tap, FR), j].reshape(FR * 64, 128) for j in range(LT)], axis=1) for tap in range(3)]
    for i in range(2):
        n = pl.ds(i * CH, CH)
        conv = dot(lhs[0], weight[0, :, n]) + dot(lhs[1], weight[1, :, n]) + dot(lhs[2], weight[2, :, n])
        conv = (conv + bias_ref[n].reshape(1, CH)).astype(jnp.bfloat16)
        for t in range(FR):
            for j in range(LT):
                oview[2 * t + i, j] = conv[t * 64:(t + 1) * 64, j * 128:(j + 1) * 128]
    o_copies = []
    for j in range(LT):
        cp = pltpu.make_async_copy(outd.at[:, j], decoded.at[0, :, :, :, pl.ds(j * 128, 128)], l_out.at[j])
        cp.start()
        o_copies.append(cp)

    own_out(0).wait()
    own_out(1).wait()
    for cp in o_copies:
        cp.wait()
    piece = rx.at[:, :, pl.ds(0, 15)]
    pltpu.make_async_copy(piece, piece, s_send).wait()
    pltpu.make_async_copy(fq, fq, s_fwd).wait()
    pltpu.make_async_copy(oc, oc, s_oc.at[0]).wait()
    pltpu.make_async_copy(lse_in, lse_in, s_oc.at[1]).wait()
    piece = rx.at[:, 0, pl.ds(0, 15)]
    pltpu.make_async_copy(piece, piece, s_o).wait()

    part = frames.at[pl.ds(2, FR), :, :, pl.ds(0, 15)]
    pltpu.make_async_copy(part, part, s_dec.at[1]).wait()

    @pl.when(g // 8 != half)
    def _():
        pltpu.make_async_copy(sendd, sendd, s_dec.at[0]).wait()

    @pl.when(g // 8 == half)
    def _():
        part = sendd.at[:, :, :, pl.ds(0, 15)]
        pltpu.make_async_copy(part, part, s_dec.at[0]).wait()
    pltpu.make_async_copy(piece, piece, r_o).wait()


def put_out(a, b, a_out, b_out, sem):
    copies = [pltpu.make_async_copy(x, o, sem.at[i]) for i, (x, o) in enumerate(((a, a_out), (b, b_out)))]
    for cp in copies:
        cp.start()
    for cp in copies:
        cp.wait()


def on_device(qkv, kv_cache, cycle_slot, valid_count, span_pos, dec_in, dec_cache, time_weight, time_bias):
    bf, f32 = jnp.bfloat16, jnp.float32
    hbm, free = pl.BlockSpec(memory_space=pltpu.MemorySpace.HBM), pl.BlockSpec(memory_space=pl.ANY)
    vmem, smem = pltpu.VMEM, pltpu.SMEM
    dma = pltpu.SemaphoreType.DMA
    operands = (
        cycle_slot, valid_count, span_pos, jnp.transpose(qkv, (1, 0, 2)), kv_cache, dec_in, dec_cache,
        time_weight, time_bias, jnp.asarray(rope_tables()),
    )
    shapes = (
        jax.ShapeDtypeStruct((TOK, 32 * HS), bf),
        jax.ShapeDtypeStruct((1, 2 * FR, 32, 2, CH), bf),
    )
    results = pl.pallas_call(
        kernel,
        out_shape=shapes,
        in_specs=[hbm] * 10,
        out_specs=(free, free),
        scratch_shapes=[
            smem((2,), jnp.int32), smem((2,), jnp.int32), smem((2,), jnp.int32),
            vmem((2, 3, HALF, TOK, HS), bf),
            vmem((HALF, TOK, HS), bf),
            vmem((4, 128, HS), bf),
            vmem((4, 128, HS), bf),
            vmem((4, 8, 128), f32),
            vmem((4, 8, 128), f32),
            vmem((2, HALF, TOK, HS), bf),
            vmem((2, 2, CYCLE, VT, HS), bf),
            vmem((3, CH, 2 * CH), bf),
            vmem((2 * CH,), f32),
            vmem((2, VT + SPANS, HS), f32),
            vmem((2, VT, HS), f32),
            vmem((2, VT, HS), f32),
            vmem((VT, HS), bf),
            vmem((2, FR, LT, 16, 2, 128), bf),
            vmem((8, 2, FR, LT, 2, 2, 128), bf),
            vmem((5, LT, 2, 16, 2, 128), bf),
            vmem((6, LT, 32, 2, 128), bf),
            dma, dma, dma((2,)), dma, dma((2,)),
            dma((HALF,)), dma, dma, dma((4,)), dma((4,)), dma((4,)), dma, dma, dma,
            dma((3,)), dma((2,)), dma, dma, dma, dma, dma((LT,)), dma((2 * LT,)), dma((LT,)),
        ],
        name="rollout",
        compiler_params=pltpu.CompilerParams(collective_id=0, has_side_effects=True, vmem_limit_bytes=20 * 1024 * 1024),
    )(
        *(pltpu.with_memory_space_constraint(x, pltpu.MemorySpace.HBM) for x in operands)
    )
    return pl.pallas_call(
        put_out,
        out_shape=shapes,
        in_specs=[free, free],
        out_specs=(hbm, hbm),
        scratch_shapes=[dma((2,))],
        name="put_out",
        compiler_params=pltpu.CompilerParams(vmem_limit_bytes=1024 * 1024),
    )(*results)


def solution(mesh):
    placed = (
        P(("grp", "sp"), None, None),
        P("grp", None, None, None, "sp"),
        P("grp"),
        P("grp"),
        P("grp"),
        P("grp", None, "sp", None, None),
        P("sp", None, None, "grp", None),
        P(),
        P(),
    )
    return jax.shard_map(
        on_device,
        mesh=mesh,
        in_specs=placed,
        out_specs=(P(("grp", "sp"), None), P("sp", None, None, "grp", None)),
        check_vma=False,
    )
```

```python
import math

import jax
import jax.numpy as jnp
import numpy as np
from jax import lax
from jax.experimental import pallas as pl
from jax.experimental.pallas import tpu as pltpu
from jax.sharding import PartitionSpec as P

HS = 128
CYCLE = 3
MESH = pl.DeviceIdType.MESH
NEG = -1e30
C2 = math.log2(math.e) / math.sqrt(HS)
HALF = 16
TOK = 32
VT = 512
SPANS = 64
FR = 3
CH = 384
LT = CH // 128


def rope_tables():
    f = np.exp(-math.log(10000.0) * np.arange(64, dtype=np.float64) / 64)
    steps = np.concatenate([np.arange(VT), VT * np.arange(SPANS)]).astype(np.float64)
    ang = steps[:, None] * np.concatenate([f, f])[None, :]
    sign = np.concatenate([-np.ones(64), np.ones(64)])
    return np.stack([np.cos(ang), np.sin(ang) * sign]).astype(np.float32)


def dot_t(a, b):
    return lax.dot_general(a, b, (((1,), (1,)), ((), ())), preferred_element_type=jnp.float32)


def dot(a, b):
    return lax.dot_general(a, b, (((1,), (0,)), ((), ())), preferred_element_type=jnp.float32)


def attend(q, parts):
    scores = [dot_t(q, k) if bias is None else dot_t(q, k) + bias for k, _, bias in parts]
    top = jnp.max(scores[0], axis=1, keepdims=True)
    for s in scores[1:]:
        top = jnp.maximum(top, jnp.max(s, axis=1, keepdims=True))
    top = top * C2
    total, acc = None, None
    for s, (_, v, _) in zip(scores, parts):
        w = jnp.exp2(s * C2 - top)
        t = jnp.sum(w, axis=1, keepdims=True)
        o = dot(w.astype(jnp.bfloat16), v)
        total = t if total is None else total + t
        acc = o if acc is None else acc + o
    return top, total, acc


def kernel(
    slot_hbm, count_hbm, pos_hbm, qkv, cache_hbm, dec_in, dec_cache, weight_hbm, bias_hbm, tab_hbm,
    out, decoded,
    slot_ref, count_ref, pos_ref, rx, fq, oc, oc_out, lse_in, lse_out, ob, cache, weight, bias_ref, tabs, cosv, sinv, kself, sendd, mid, frames, outd,
    s_send, s_fwd, s_oc, s_o, s_dec, r_qb, r_a, r_b, r_fq, r_oc, r_lse, r_o, r_dec, r_mid, l_state, l_own, l_cache, l_w, l_bias, l_tab, l_dc, l_ds, l_out,
):
    g = lax.axis_index("grp")
    s = lax.axis_index("sp")
    half = s // HALF
    me = s % HALF
    y = me // 2
    c = me % 2
    partner = (s + HALF) % 32
    other = 1 - half

    def peer(k, cc):
        step = jnp.where(k == 0, 4, ((8 - k) // 2) * (1 - 2 * (k % 2)))
        return ((y + step + 8) % 8) * 2 + (c + cc) % 2

    def for_peers(fn):
        def body(i, _):
            fn(peer(i // 2, i % 2))
            return 0
        lax.fori_loop(0, 14, body, 0)
        fn(y * 2 + (1 - c))

    bar = pltpu.get_barrier_semaphore()
    for_peers(lambda t: pl.semaphore_signal(bar, 1, device_id=(g, half * HALF + t), device_id_type=MESH))
    def greet(i, _):
        pl.semaphore_signal(bar, 1, device_id=((g + 1 + i) % 16, s), device_id_type=MESH)
        return 0

    @pl.when(half == 1)
    def _():
        lax.fori_loop(0, 15, greet, 0)

    def cols(h):
        return pl.ds(pl.multiple_of(h * HS, HS), HS)

    head = (s, partner)
    own = [pltpu.make_async_copy(qkv.at[:, :, cols(head[j])], rx.at[j, :, me], l_own.at[j]) for j in range(2)]
    for cp in own:
        cp.start()
    c_state = [
        pltpu.make_async_copy(h, r, l_state.at[i])
        for i, (h, r) in enumerate(((slot_hbm, slot_ref), (count_hbm, count_ref), (pos_hbm, pos_ref)))
    ]
    for cp in c_state:
        cp.start()
    c_tab = pltpu.make_async_copy(tab_hbm, tabs, l_tab)
    c_tab.start()
    ds_copies = []
    for v in range(2):
        for j in range(LT):
            cp = pltpu.make_async_copy(dec_in.at[v, :, 0, :, pl.ds(j * 128, 128)], sendd.reshape(2, FR, LT, 32, 128).at[v, :, j], l_ds.at[v * LT + j])
            cp.start()
            ds_copies.append(cp)
    c_cache = pltpu.make_async_copy(cache_hbm, cache, l_cache)
    c_cache.start()
    dc_copies = []
    for j in range(LT):
        cp = pltpu.make_async_copy(dec_cache.at[0, :, :, :, pl.ds(j * 128, 128)], frames.reshape(5, LT, 32, 2, 128).at[pl.ds(0, 2), j], l_dc.at[j])
        cp.start()
        dc_copies.append(cp)
    c_w = pltpu.make_async_copy(weight_hbm, weight, l_w)
    c_w.start()
    c_b = pltpu.make_async_copy(bias_hbm, bias_ref, l_bias)
    c_b.start()

    pl.semaphore_wait(bar, 15 + 31 * half)

    def report(i, _):
        pl.semaphore_signal(bar, 1, device_id=((g + i) % 16, partner), device_id_type=MESH)
        return 0

    @pl.when(half == 0)
    def _():
        lax.fori_loop(0, 16, report, 0)

    @pl.when(half == 1)
    def _():
        pl.semaphore_signal(bar, 1, device_id=(g, partner), device_id_type=MESH)

    def send(part, n, j, t, rsem):
        pltpu.make_async_remote_copy(
            qkv.at[pl.ds(part, n), :, cols(half * HALF + t if j == 0 else other * HALF + t)],
            rx.at[j, pl.ds(part, n), me], s_send, rsem,
            device_id=(g, half * HALF + t), device_id_type=MESH,
        ).start()

    for_peers(lambda t: send(0, 1, 1, t, r_qb.at[me]))
    for_peers(lambda t: send(0, 3, 0, t, r_a))
    for_peers(lambda t: send(1, 2, 1, t, r_b))

    c_tab.wait()
    for cp in c_state:
        cp.wait()
    bases = [[tabs[i, pl.ds(VT + pos_ref[v], 1), :] for i in range(2)] for v in range(2)]

    def make_tables(i, _):
        rows = pl.ds(pl.multiple_of(i * 128, 128), 128)
        ct, st = tabs[0, rows, :], tabs[1, rows, :]
        for v in range(2):
            cb, sb = bases[v]
            cosv[v, rows, :] = ct * cb - st * sb
            sinv[v, rows, :] = st * cb + ct * sb
        return 0
    lax.fori_loop(0, 4, make_tables, 0)

    def rotate(x, v, row, n):
        x = x.astype(jnp.float32)
        rows = pl.ds(pl.multiple_of(row, n), n)
        return (x * cosv[v, rows, :] + pltpu.roll(x, 64, 1) * sinv[v, rows, :]).astype(jnp.bfloat16)

    @pl.when(half == 0)
    def _():
        pl.semaphore_wait(bar, 1)

    for cp in ds_copies:
        cp.wait()

    def send_stage(i, _):
        gd, sd = (g + i) % 16, (g // 8) * HALF + me
        src, dst = sendd.at[:, :, :, gd], mid.at[g % 8, :, :, :, half]
        itself = (gd == g) & (sd == s)

        @pl.when(jnp.logical_not(itself))
        def _():
            pltpu.make_async_remote_copy(src, dst, s_dec.at[0], r_mid, device_id=(gd, sd), device_id_type=MESH).start()

        @pl.when(itself)
        def _():
            pltpu.make_async_copy(src, dst, r_mid).start()
        return 0

    @pl.when((half == 1) | (g // 8 == 0))
    def _():
        lax.fori_loop(0, 16, send_stage, 0)

    def forward(t):
        pltpu.make_async_remote_copy(
            rx.at[1, 0, t], fq.at[t], s_fwd, r_fq.at[t // 4],
            device_id=(g, partner), device_id_type=MESH,
        ).start()

    for cp in own:
        cp.wait()
    def far_chunk(k):
        return (k + y // 2 + 2) % 4

    def wait_forward(t):
        @pl.when(t != me)
        def _():
            pltpu.make_async_copy(rx.at[1, 0, t], rx.at[1, 0, t], r_qb.at[t]).wait()
        forward(t)

    def forward_chunks(k, _):
        wait_forward(far_chunk(k // 4) * 4 + k % 4)
        return 0

    @pl.when(half == 0)
    def _():
        lax.fori_loop(0, 16, forward_chunks, 0)

    @pl.when(half == 1)
    def _():
        forward(me)
        for_peers(wait_forward)

    @pl.when((half == 0) & (g // 8 == 1))
    def _():
        lax.fori_loop(0, 16, send_stage, 0)

    eye = lax.broadcasted_iota(jnp.int32, (128, 128), 0) == lax.broadcasted_iota(jnp.int32, (128, 128), 1)

    def slots(v):
        cs, vc = slot_ref[v], count_ref[v]
        s0 = jnp.where(cs == 0, 1, 0)
        s1 = jnp.where(cs == 2, 1, 2)
        return [(sl, jnp.where(sl < vc, 0.0, NEG)) for sl in (s0, s1)]

    def send_out(j, t):
        pltpu.make_async_remote_copy(
            ob.at[j, t], out.at[:, cols(head[j])], s_o, r_o,
            device_id=(g, half * HALF + t), device_id_type=MESH,
        ).start()

    def own_out(j):
        return pltpu.make_async_copy(ob.at[j, me], out.at[:, cols(head[j])], l_own.at[j])

    def rotate_keys(j):
        def body(i, _):
            kself[pl.ds(pl.multiple_of(i * 128, 128), 128), :] = rotate(rx[j, 1, pl.ds(i * 4, 4)].reshape(128, HS), half, i * 128, 128)
            return 0
        lax.fori_loop(0, 4, body, 0)

    def serve_partner():
        there = slots(other)

        def cross(k, _):
            i = far_chunk(k)
            pltpu.make_async_copy(fq.at[pl.ds(i * 4, 4)], fq.at[pl.ds(i * 4, 4)], r_fq.at[i]).wait()
            q = rotate(fq[pl.ds(i * 4, 4)].reshape(128, HS), other, i * 128, 128)
            top, total, acc = attend(q, [(cache[other, 0, sl], cache[other, 1, sl], b) for sl, b in there])
            oc_out[i] = (acc / total).astype(jnp.bfloat16)
            lse = jnp.broadcast_to(top + jnp.log2(total), (128, 128))
            lse_out[i] = jnp.sum(jnp.where(eye, lse, 0.0), axis=0, keepdims=True)
            pltpu.make_async_remote_copy(oc_out.at[i], oc.at[i], s_oc.at[0], r_oc.at[i], device_id=(g, partner), device_id_type=MESH).start()
            pltpu.make_async_remote_copy(lse_out.at[i], lse_in.at[i], s_oc.at[1], r_lse.at[i], device_id=(g, partner), device_id_type=MESH).start()
            return 0
        lax.fori_loop(0, 4, cross, 0)

    def own_head():
        pltpu.make_async_copy(rx.at[0, :, pl.ds(0, 15)], rx.at[0, :, pl.ds(0, 15)], r_a).wait()
        here = slots(half)
        rotate_keys(0)

        def whole(i, _):
            q = rotate(rx[0, 0, pl.ds(i * 8, 8)].reshape(256, HS), half, i * 256, 256)
            parts = [(cache[half, 0, sl], cache[half, 1, sl], b) for sl, b in here]
            parts.append((kself[...], rx[0, 2].reshape(VT, HS), None))
            top, total, acc = attend(q, parts)
            ob[0, pl.ds(i * 8, 8)] = (acc / total).astype(jnp.bfloat16).reshape(8, TOK, HS)
            return 0
        lax.fori_loop(0, 2, whole, 0)
        for_peers(lambda t: send_out(0, t))
        own_out(0).start()

    c_cache.wait()

    @pl.when(half == 1)
    def _():
        serve_partner()

    @pl.when(half == 0)
    def _():
        own_head()

    @pl.when(half == 1)
    def _():
        own_head()

    @pl.when(half == 0)
    def _():
        serve_partner()

    pltpu.make_async_copy(mid, mid, r_mid).wait()
    fresh = frames.at[pl.ds(2, FR)]

    def send_frames(t):
        pltpu.make_async_remote_copy(
            mid.at[t // 2, t % 2], fresh.at[:, :, :, me], s_dec.at[1], r_dec,
            device_id=(g, half * HALF + t), device_id_type=MESH,
        ).start()
    for_peers(send_frames)
    pltpu.make_async_copy(mid.at[me // 2, me % 2], fresh.at[:, :, :, me], r_dec).start()

    pltpu.make_async_copy(rx.at[1, pl.ds(1, 2), pl.ds(0, 15)], rx.at[1, pl.ds(1, 2), pl.ds(0, 15)], r_b).wait()
    rotate_keys(1)

    def merged(k, _):
        i = far_chunk(k)
        q = rotate(rx[1, 0, pl.ds(i * 4, 4)].reshape(128, HS), half, i * 128, 128)
        top, total, acc = attend(q, [(kself[...], rx[1, 2].reshape(VT, HS), None)])
        pltpu.make_async_copy(lse_in.at[i], lse_in.at[i], r_lse.at[i]).wait()
        pltpu.make_async_copy(oc.at[i], oc.at[i], r_oc.at[i]).wait()
        lse = jnp.broadcast_to(lse_in[i], (128, 128))
        lse = jnp.sum(jnp.where(eye, lse, 0.0), axis=1, keepdims=True)
        both = jnp.maximum(lse, top)
        wc = jnp.exp2(lse - both)
        ws = jnp.exp2(top - both)
        mixed = (oc[i].astype(jnp.float32) * wc + acc * ws) / (wc + total * ws)
        ob[1, pl.ds(i * 4, 4)] = mixed.astype(jnp.bfloat16).reshape(4, TOK, HS)

        def hand_out(b, _):
            t = i * 4 + b

            @pl.when(t != me)
            def _():
                send_out(1, t)

            @pl.when(t == me)
            def _():
                own_out(1).start()
            return 0
        lax.fori_loop(0, 4, hand_out, 0)
        return 0
    lax.fori_loop(0, 4, merged, 0)

    for cp in dc_copies:
        cp.wait()
    c_w.wait()
    c_b.wait()
    pltpu.make_async_copy(fresh, fresh, r_dec).wait()
    fview = frames.reshape(5, LT, 64, 128)
    oview = outd.reshape(6, LT, 64, 128)
    lhs = [jnp.concatenate([fview[pl.ds(tap, FR), j].reshape(FR * 64, 128) for j in range(LT)], axis=1) for tap in range(3)]
    for i in range(2):
        n = pl.ds(i * CH, CH)
        conv = dot(lhs[0], weight[0, :, n]) + dot(lhs[1], weight[1, :, n]) + dot(lhs[2], weight[2, :, n])
        conv = (conv + bias_ref[n].reshape(1, CH)).astype(jnp.bfloat16)
        for t in range(FR):
            for j in range(LT):
                oview[2 * t + i, j] = conv[t * 64:(t + 1) * 64, j * 128:(j + 1) * 128]
    o_copies = []
    for j in range(LT):
        cp = pltpu.make_async_copy(outd.at[:, j], decoded.at[0, :, :, :, pl.ds(j * 128, 128)], l_out.at[j])
        cp.start()
        o_copies.append(cp)

    own_out(0).wait()
    own_out(1).wait()
    for cp in o_copies:
        cp.wait()
    piece = rx.at[:, :, pl.ds(0, 15)]
    pltpu.make_async_copy(piece, piece, s_send).wait()
    pltpu.make_async_copy(fq, fq, s_fwd).wait()
    pltpu.make_async_copy(oc, oc, s_oc.at[0]).wait()
    pltpu.make_async_copy(lse_in, lse_in, s_oc.at[1]).wait()
    piece = rx.at[:, 0, pl.ds(0, 15)]
    pltpu.make_async_copy(piece, piece, s_o).wait()

    part = frames.at[pl.ds(2, FR), :, :, pl.ds(0, 15)]
    pltpu.make_async_copy(part, part, s_dec.at[1]).wait()

    @pl.when(g // 8 != half)
    def _():
        pltpu.make_async_copy(sendd, sendd, s_dec.at[0]).wait()

    @pl.when(g // 8 == half)
    def _():
        part = sendd.at[:, :, :, pl.ds(0, 15)]
        pltpu.make_async_copy(part, part, s_dec.at[0]).wait()
    pltpu.make_async_copy(piece, piece, r_o).wait()


def put_out(a, b, a_out, b_out, sem):
    copies = [pltpu.make_async_copy(x, o, sem.at[i]) for i, (x, o) in enumerate(((a, a_out), (b, b_out)))]
    for cp in copies:
        cp.start()
    for cp in copies:
        cp.wait()


def on_device(qkv, kv_cache, cycle_slot, valid_count, span_pos, dec_in, dec_cache, time_weight, time_bias):
    bf, f32 = jnp.bfloat16, jnp.float32
    hbm, free = pl.BlockSpec(memory_space=pltpu.MemorySpace.HBM), pl.BlockSpec(memory_space=pl.ANY)
    vmem, smem = pltpu.VMEM, pltpu.SMEM
    dma = pltpu.SemaphoreType.DMA
    operands = (
        cycle_slot, valid_count, span_pos, jnp.transpose(qkv, (1, 0, 2)), kv_cache, dec_in, dec_cache,
        time_weight, time_bias, jnp.asarray(rope_tables()),
    )
    shapes = (
        jax.ShapeDtypeStruct((TOK, 32 * HS), bf),
        jax.ShapeDtypeStruct((1, 2 * FR, 32, 2, CH), bf),
    )
    results = pl.pallas_call(
        kernel,
        out_shape=shapes,
        in_specs=[hbm] * 10,
        out_specs=(free, free),
        scratch_shapes=[
            smem((2,), jnp.int32), smem((2,), jnp.int32), smem((2,), jnp.int32),
            vmem((2, 3, HALF, TOK, HS), bf),
            vmem((HALF, TOK, HS), bf),
            vmem((4, 128, HS), bf),
            vmem((4, 128, HS), bf),
            vmem((4, 1, 128), f32),
            vmem((4, 1, 128), f32),
            vmem((2, HALF, TOK, HS), bf),
            vmem((2, 2, CYCLE, VT, HS), bf),
            vmem((3, CH, 2 * CH), bf),
            vmem((2 * CH,), f32),
            vmem((2, VT + SPANS, HS), f32),
            vmem((2, VT, HS), f32),
            vmem((2, VT, HS), f32),
            vmem((VT, HS), bf),
            vmem((2, FR, LT, 16, 2, 128), bf),
            vmem((8, 2, FR, LT, 2, 2, 128), bf),
            vmem((5, LT, 2, 16, 2, 128), bf),
            vmem((6, LT, 32, 2, 128), bf),
            dma, dma, dma((2,)), dma, dma((2,)),
            dma((HALF,)), dma, dma, dma((4,)), dma((4,)), dma((4,)), dma, dma, dma,
            dma((3,)), dma((2,)), dma, dma, dma, dma, dma((LT,)), dma((2 * LT,)), dma((LT,)),
        ],
        name="rollout",
        compiler_params=pltpu.CompilerParams(collective_id=0, has_side_effects=True, vmem_limit_bytes=20 * 1024 * 1024),
    )(
        *(pltpu.with_memory_space_constraint(x, pltpu.MemorySpace.HBM) for x in operands)
    )
    return pl.pallas_call(
        put_out,
        out_shape=shapes,
        in_specs=[free, free],
        out_specs=(hbm, hbm),
        scratch_shapes=[dma((2,))],
        name="put_out",
        compiler_params=pltpu.CompilerParams(vmem_limit_bytes=1024 * 1024),
    )(*results)


def solution(mesh):
    placed = (
        P(("grp", "sp"), None, None),
        P("grp", None, None, None, "sp"),
        P("grp"),
        P("grp"),
        P("grp"),
        P("grp", None, "sp", None, None),
        P("sp", None, None, "grp", None),
        P(),
        P(),
    )
    return jax.shard_map(
        on_device,
        mesh=mesh,
        in_specs=placed,
        out_specs=(P(("grp", "sp"), None), P("sp", None, None, "grp", None)),
        check_vma=False,
    )
```

```python
import math

import jax
import jax.numpy as jnp
import numpy as np
from jax import lax
from jax.experimental import pallas as pl
from jax.experimental.pallas import tpu as pltpu
from jax.sharding import PartitionSpec as P

HS = 128
CYCLE = 3
MESH = pl.DeviceIdType.MESH
NEG = -1e30
C2 = math.log2(math.e) / math.sqrt(HS)
HALF = 16
TOK = 32
VT = 512
SPANS = 64
FR = 3
CH = 384
LT = CH // 128


def rope_tables():
    f = np.exp(-math.log(10000.0) * np.arange(64, dtype=np.float64) / 64)
    steps = np.concatenate([np.arange(VT), VT * np.arange(SPANS)]).astype(np.float64)
    ang = steps[:, None] * np.concatenate([f, f])[None, :]
    sign = np.concatenate([-np.ones(64), np.ones(64)])
    return np.stack([np.cos(ang), np.sin(ang) * sign]).astype(np.float32)


def dot_t(a, b):
    return lax.dot_general(a, b, (((1,), (1,)), ((), ())), preferred_element_type=jnp.float32)


def dot(a, b):
    return lax.dot_general(a, b, (((1,), (0,)), ((), ())), preferred_element_type=jnp.float32)


def attend(q, parts):
    scores = [dot_t(q, k) if bias is None else dot_t(q, k) + bias for k, _, bias in parts]
    top = jnp.max(scores[0], axis=1, keepdims=True)
    for s in scores[1:]:
        top = jnp.maximum(top, jnp.max(s, axis=1, keepdims=True))
    top = top * C2
    total, acc = None, None
    for s, (_, v, _) in zip(scores, parts):
        w = jnp.exp2(s * C2 - top)
        t = jnp.sum(w, axis=1, keepdims=True)
        o = dot(w.astype(jnp.bfloat16), v)
        total = t if total is None else total + t
        acc = o if acc is None else acc + o
    return top, total, acc


def kernel(
    slot_hbm, count_hbm, pos_hbm, qkv, cache_hbm, dec_in, dec_cache, weight_hbm, bias_hbm, tab_hbm,
    out, decoded,
    slot_ref, count_ref, pos_ref, rx, fq, oc, oc_out, lse_in, lse_out, ob, cache, weight, bias_ref, tabs, cosv, sinv, kself, sendd, mid, frames, outd,
    s_send, s_fwd, s_oc, s_o, s_dec, r_qb, r_a, r_b, r_fq, r_oc, r_lse, r_o, r_dec, r_mid, l_state, l_own, l_cache, l_w, l_bias, l_tab, l_dc, l_ds, l_out,
):
    g = lax.axis_index("grp")
    s = lax.axis_index("sp")
    half = s // HALF
    me = s % HALF
    y = me // 2
    c = me % 2
    partner = (s + HALF) % 32
    other = 1 - half

    def peer(k, cc):
        step = jnp.where(k == 0, 4, ((8 - k) // 2) * (1 - 2 * (k % 2)))
        return ((y + step + 8) % 8) * 2 + (c + cc) % 2

    def for_peers(fn):
        def body(i, _):
            fn(peer(i // 2, i % 2))
            return 0
        lax.fori_loop(0, 14, body, 0)
        fn(y * 2 + (1 - c))

    bar = pltpu.get_barrier_semaphore()
    for_peers(lambda t: pl.semaphore_signal(bar, 1, device_id=(g, half * HALF + t), device_id_type=MESH))
    def greet(i, _):
        pl.semaphore_signal(bar, 1, device_id=((g + 1 + i) % 16, s), device_id_type=MESH)
        return 0

    @pl.when(half == 1)
    def _():
        lax.fori_loop(0, 15, greet, 0)

    def cols(h):
        return pl.ds(pl.multiple_of(h * HS, HS), HS)

    head = (s, partner)
    own = [pltpu.make_async_copy(qkv.at[:, :, cols(head[j])], rx.at[j, :, me], l_own.at[j]) for j in range(2)]
    for cp in own:
        cp.start()
    c_state = [
        pltpu.make_async_copy(h, r, l_state.at[i])
        for i, (h, r) in enumerate(((slot_hbm, slot_ref), (count_hbm, count_ref), (pos_hbm, pos_ref)))
    ]
    for cp in c_state:
        cp.start()
    c_tab = pltpu.make_async_copy(tab_hbm, tabs, l_tab)
    c_tab.start()
    ds_copies = []
    for v in range(2):
        for j in range(LT):
            cp = pltpu.make_async_copy(dec_in.at[v, :, 0, :, pl.ds(j * 128, 128)], sendd.reshape(2, FR, LT, 32, 128).at[v, :, j], l_ds.at[v * LT + j])
            cp.start()
            ds_copies.append(cp)
    c_cache = pltpu.make_async_copy(cache_hbm, cache, l_cache)
    c_cache.start()
    dc_copies = []
    for j in range(LT):
        cp = pltpu.make_async_copy(dec_cache.at[0, :, :, :, pl.ds(j * 128, 128)], frames.reshape(5, LT, 32, 2, 128).at[pl.ds(0, 2), j], l_dc.at[j])
        cp.start()
        dc_copies.append(cp)
    c_w = pltpu.make_async_copy(weight_hbm, weight, l_w)
    c_w.start()
    c_b = pltpu.make_async_copy(bias_hbm, bias_ref, l_bias)
    c_b.start()

    pl.semaphore_wait(bar, 15 + 31 * half)

    def report(i, _):
        pl.semaphore_signal(bar, 1, device_id=((g + i) % 16, partner), device_id_type=MESH)
        return 0

    @pl.when(half == 0)
    def _():
        lax.fori_loop(0, 16, report, 0)

    @pl.when(half == 1)
    def _():
        pl.semaphore_signal(bar, 1, device_id=(g, partner), device_id_type=MESH)

    def send(part, n, j, t, rsem):
        pltpu.make_async_remote_copy(
            qkv.at[pl.ds(part, n), :, cols(half * HALF + t if j == 0 else other * HALF + t)],
            rx.at[j, pl.ds(part, n), me], s_send, rsem,
            device_id=(g, half * HALF + t), device_id_type=MESH,
        ).start()

    for_peers(lambda t: send(0, 1, 1, t, r_qb.at[me]))
    for_peers(lambda t: send(0, 3, 0, t, r_a))
    for_peers(lambda t: send(1, 2, 1, t, r_b))

    for cp in ds_copies:
        cp.wait()

    def send_stage(i, _):
        gd, sd = (g + i) % 16, (g // 8) * HALF + me
        src, dst = sendd.at[:, :, :, gd], mid.at[g % 8, :, :, :, half]
        itself = (gd == g) & (sd == s)

        @pl.when(jnp.logical_not(itself))
        def _():
            pltpu.make_async_remote_copy(src, dst, s_dec.at[0], r_mid, device_id=(gd, sd), device_id_type=MESH).start()

        @pl.when(itself)
        def _():
            pltpu.make_async_copy(src, dst, r_mid).start()
        return 0

    @pl.when(half == 1)
    def _():
        lax.fori_loop(0, 16, send_stage, 0)

    c_tab.wait()
    for cp in c_state:
        cp.wait()
    bases = [[tabs[i, pl.ds(VT + pos_ref[v], 1), :] for i in range(2)] for v in range(2)]

    def make_tables(i, _):
        rows = pl.ds(pl.multiple_of(i * 128, 128), 128)
        ct, st = tabs[0, rows, :], tabs[1, rows, :]
        for v in range(2):
            cb, sb = bases[v]
            cosv[v, rows, :] = ct * cb - st * sb
            sinv[v, rows, :] = st * cb + ct * sb
        return 0
    lax.fori_loop(0, 4, make_tables, 0)

    def rotate(x, v, row, n):
        x = x.astype(jnp.float32)
        rows = pl.ds(pl.multiple_of(row, n), n)
        return (x * cosv[v, rows, :] + pltpu.roll(x, 64, 1) * sinv[v, rows, :]).astype(jnp.bfloat16)

    @pl.when(half == 0)
    def _():
        pl.semaphore_wait(bar, 1)

    @pl.when((half == 0) & (g // 8 == 0))
    def _():
        lax.fori_loop(0, 16, send_stage, 0)

    def forward(t):
        pltpu.make_async_remote_copy(
            rx.at[1, 0, t], fq.at[t], s_fwd, r_fq.at[t // 4],
            device_id=(g, partner), device_id_type=MESH,
        ).start()

    for cp in own:
        cp.wait()
    def far_chunk(k):
        return (k + y // 2 + 2) % 4

    def wait_forward(t):
        @pl.when(t != me)
        def _():
            pltpu.make_async_copy(rx.at[1, 0, t], rx.at[1, 0, t], r_qb.at[t]).wait()
        forward(t)

    def forward_chunks(k, _):
        wait_forward(far_chunk(k // 4) * 4 + k % 4)
        return 0

    @pl.when(half == 0)
    def _():
        lax.fori_loop(0, 16, forward_chunks, 0)

    @pl.when(half == 1)
    def _():
        forward(me)
        for_peers(wait_forward)

    @pl.when((half == 0) & (g // 8 == 1))
    def _():
        lax.fori_loop(0, 16, send_stage, 0)

    eye = lax.broadcasted_iota(jnp.int32, (128, 128), 0) == lax.broadcasted_iota(jnp.int32, (128, 128), 1)

    def slots(v):
        cs, vc = slot_ref[v], count_ref[v]
        s0 = jnp.where(cs == 0, 1, 0)
        s1 = jnp.where(cs == 2, 1, 2)
        return [(sl, jnp.where(sl < vc, 0.0, NEG)) for sl in (s0, s1)]

    def send_out(j, t):
        pltpu.make_async_remote_copy(
            ob.at[j, t], out.at[:, cols(head[j])], s_o, r_o,
            device_id=(g, half * HALF + t), device_id_type=MESH,
        ).start()

    def own_out(j):
        return pltpu.make_async_copy(ob.at[j, me], out.at[:, cols(head[j])], l_own.at[j])

    def rotate_keys(j):
        def body(i, _):
            kself[pl.ds(pl.multiple_of(i * 128, 128), 128), :] = rotate(rx[j, 1, pl.ds(i * 4, 4)].reshape(128, HS), half, i * 128, 128)
            return 0
        lax.fori_loop(0, 4, body, 0)

    def serve_partner():
        there = slots(other)

        def cross(k, _):
            i = far_chunk(k)
            pltpu.make_async_copy(fq.at[pl.ds(i * 4, 4)], fq.at[pl.ds(i * 4, 4)], r_fq.at[i]).wait()
            q = rotate(fq[pl.ds(i * 4, 4)].reshape(128, HS), other, i * 128, 128)
            top, total, acc = attend(q, [(cache[other, 0, sl], cache[other, 1, sl], b) for sl, b in there])
            oc_out[i] = (acc / total).astype(jnp.bfloat16)
            lse = jnp.broadcast_to(top + jnp.log2(total), (128, 128))
            lse_out[i] = jnp.sum(jnp.where(eye, lse, 0.0), axis=0, keepdims=True)
            pltpu.make_async_remote_copy(oc_out.at[i], oc.at[i], s_oc.at[0], r_oc.at[i], device_id=(g, partner), device_id_type=MESH).start()
            pltpu.make_async_remote_copy(lse_out.at[i], lse_in.at[i], s_oc.at[1], r_lse.at[i], device_id=(g, partner), device_id_type=MESH).start()
            return 0
        lax.fori_loop(0, 4, cross, 0)

    def own_head():
        pltpu.make_async_copy(rx.at[0, :, pl.ds(0, 15)], rx.at[0, :, pl.ds(0, 15)], r_a).wait()
        here = slots(half)
        rotate_keys(0)

        def whole(i, _):
            q = rotate(rx[0, 0, pl.ds(i * 8, 8)].reshape(256, HS), half, i * 256, 256)
            parts = [(cache[half, 0, sl], cache[half, 1, sl], b) for sl, b in here]
            parts.append((kself[...], rx[0, 2].reshape(VT, HS), None))
            top, total, acc = attend(q, parts)
            ob[0, pl.ds(i * 8, 8)] = (acc / total).astype(jnp.bfloat16).reshape(8, TOK, HS)
            return 0
        lax.fori_loop(0, 2, whole, 0)
        for_peers(lambda t: send_out(0, t))
        own_out(0).start()

    c_cache.wait()

    @pl.when(half == 1)
    def _():
        serve_partner()

    @pl.when(half == 0)
    def _():
        own_head()

    @pl.when(half == 1)
    def _():
        own_head()

    @pl.when(half == 0)
    def _():
        serve_partner()

    pltpu.make_async_copy(mid, mid, r_mid).wait()
    fresh = frames.at[pl.ds(2, FR)]

    def send_frames(t):
        pltpu.make_async_remote_copy(
            mid.at[t // 2, t % 2], fresh.at[:, :, :, me], s_dec.at[1], r_dec,
            device_id=(g, half * HALF + t), device_id_type=MESH,
        ).start()
    for_peers(send_frames)
    pltpu.make_async_copy(mid.at[me // 2, me % 2], fresh.at[:, :, :, me], r_dec).start()

    pltpu.make_async_copy(rx.at[1, pl.ds(1, 2), pl.ds(0, 15)], rx.at[1, pl.ds(1, 2), pl.ds(0, 15)], r_b).wait()
    rotate_keys(1)

    def merged(k, _):
        i = far_chunk(k)
        q = rotate(rx[1, 0, pl.ds(i * 4, 4)].reshape(128, HS), half, i * 128, 128)
        top, total, acc = attend(q, [(kself[...], rx[1, 2].reshape(VT, HS), None)])
        pltpu.make_async_copy(lse_in.at[i], lse_in.at[i], r_lse.at[i]).wait()
        pltpu.make_async_copy(oc.at[i], oc.at[i], r_oc.at[i]).wait()
        lse = jnp.broadcast_to(lse_in[i], (128, 128))
        lse = jnp.sum(jnp.where(eye, lse, 0.0), axis=1, keepdims=True)
        both = jnp.maximum(lse, top)
        wc = jnp.exp2(lse - both)
        ws = jnp.exp2(top - both)
        mixed = (oc[i].astype(jnp.float32) * wc + acc * ws) / (wc + total * ws)
        ob[1, pl.ds(i * 4, 4)] = mixed.astype(jnp.bfloat16).reshape(4, TOK, HS)

        def hand_out(b, _):
            t = i * 4 + b

            @pl.when(t != me)
            def _():
                send_out(1, t)

            @pl.when(t == me)
            def _():
                own_out(1).start()
            return 0
        lax.fori_loop(0, 4, hand_out, 0)
        return 0
    lax.fori_loop(0, 4, merged, 0)

    for cp in dc_copies:
        cp.wait()
    c_w.wait()
    c_b.wait()
    pltpu.make_async_copy(fresh, fresh, r_dec).wait()
    fview = frames.reshape(5, LT, 64, 128)
    oview = outd.reshape(6, LT, 64, 128)
    lhs = [jnp.concatenate([fview[pl.ds(tap, FR), j].reshape(FR * 64, 128) for j in range(LT)], axis=1) for tap in range(3)]
    for i in range(2):
        n = pl.ds(i * CH, CH)
        conv = dot(lhs[0], weight[0, :, n]) + dot(lhs[1], weight[1, :, n]) + dot(lhs[2], weight[2, :, n])
        conv = (conv + bias_ref[n].reshape(1, CH)).astype(jnp.bfloat16)
        for t in range(FR):
            for j in range(LT):
                oview[2 * t + i, j] = conv[t * 64:(t + 1) * 64, j * 128:(j + 1) * 128]
    o_copies = []
    for j in range(LT):
        cp = pltpu.make_async_copy(outd.at[:, j], decoded.at[0, :, :, :, pl.ds(j * 128, 128)], l_out.at[j])
        cp.start()
        o_copies.append(cp)

    own_out(0).wait()
    own_out(1).wait()
    for cp in o_copies:
        cp.wait()
    piece = rx.at[:, :, pl.ds(0, 15)]
    pltpu.make_async_copy(piece, piece, s_send).wait()
    pltpu.make_async_copy(fq, fq, s_fwd).wait()
    pltpu.make_async_copy(oc, oc, s_oc.at[0]).wait()
    pltpu.make_async_copy(lse_in, lse_in, s_oc.at[1]).wait()
    piece = rx.at[:, 0, pl.ds(0, 15)]
    pltpu.make_async_copy(piece, piece, s_o).wait()

    part = frames.at[pl.ds(2, FR), :, :, pl.ds(0, 15)]
    pltpu.make_async_copy(part, part, s_dec.at[1]).wait()

    @pl.when(g // 8 != half)
    def _():
        pltpu.make_async_copy(sendd, sendd, s_dec.at[0]).wait()

    @pl.when(g // 8 == half)
    def _():
        part = sendd.at[:, :, :, pl.ds(0, 15)]
        pltpu.make_async_copy(part, part, s_dec.at[0]).wait()
    pltpu.make_async_copy(piece, piece, r_o).wait()


def put_out(a, b, a_out, b_out, sem):
    copies = [pltpu.make_async_copy(x, o, sem.at[i]) for i, (x, o) in enumerate(((a, a_out), (b, b_out)))]
    for cp in copies:
        cp.start()
    for cp in copies:
        cp.wait()


def on_device(qkv, kv_cache, cycle_slot, valid_count, span_pos, dec_in, dec_cache, time_weight, time_bias):
    bf, f32 = jnp.bfloat16, jnp.float32
    hbm, free = pl.BlockSpec(memory_space=pltpu.MemorySpace.HBM), pl.BlockSpec(memory_space=pl.ANY)
    vmem, smem = pltpu.VMEM, pltpu.SMEM
    dma = pltpu.SemaphoreType.DMA
    operands = (
        cycle_slot, valid_count, span_pos, jnp.transpose(qkv, (1, 0, 2)), kv_cache, dec_in, dec_cache,
        time_weight, time_bias, jnp.asarray(rope_tables()),
    )
    shapes = (
        jax.ShapeDtypeStruct((TOK, 32 * HS), bf),
        jax.ShapeDtypeStruct((1, 2 * FR, 32, 2, CH), bf),
    )
    results = pl.pallas_call(
        kernel,
        out_shape=shapes,
        in_specs=[hbm] * 10,
        out_specs=(free, free),
        scratch_shapes=[
            smem((2,), jnp.int32), smem((2,), jnp.int32), smem((2,), jnp.int32),
            vmem((2, 3, HALF, TOK, HS), bf),
            vmem((HALF, TOK, HS), bf),
            vmem((4, 128, HS), bf),
            vmem((4, 128, HS), bf),
            vmem((4, 1, 128), f32),
            vmem((4, 1, 128), f32),
            vmem((2, HALF, TOK, HS), bf),
            vmem((2, 2, CYCLE, VT, HS), bf),
            vmem((3, CH, 2 * CH), bf),
            vmem((2 * CH,), f32),
            vmem((2, VT + SPANS, HS), f32),
            vmem((2, VT, HS), f32),
            vmem((2, VT, HS), f32),
            vmem((VT, HS), bf),
            vmem((2, FR, LT, 16, 2, 128), bf),
            vmem((8, 2, FR, LT, 2, 2, 128), bf),
            vmem((5, LT, 2, 16, 2, 128), bf),
            vmem((6, LT, 32, 2, 128), bf),
            dma, dma, dma((2,)), dma, dma((2,)),
            dma((HALF,)), dma, dma, dma((4,)), dma((4,)), dma((4,)), dma, dma, dma,
            dma((3,)), dma((2,)), dma, dma, dma, dma, dma((LT,)), dma((2 * LT,)), dma((LT,)),
        ],
        name="rollout",
        compiler_params=pltpu.CompilerParams(collective_id=0, has_side_effects=True, vmem_limit_bytes=20 * 1024 * 1024),
    )(
        *(pltpu.with_memory_space_constraint(x, pltpu.MemorySpace.HBM) for x in operands)
    )
    return pl.pallas_call(
        put_out,
        out_shape=shapes,
        in_specs=[free, free],
        out_specs=(hbm, hbm),
        scratch_shapes=[dma((2,))],
        name="put_out",
        compiler_params=pltpu.CompilerParams(vmem_limit_bytes=1024 * 1024),
    )(*results)


def solution(mesh):
    placed = (
        P(("grp", "sp"), None, None),
        P("grp", None, None, None, "sp"),
        P("grp"),
        P("grp"),
        P("grp"),
        P("grp", None, "sp", None, None),
        P("sp", None, None, "grp", None),
        P(),
        P(),
    )
    return jax.shard_map(
        on_device,
        mesh=mesh,
        in_specs=placed,
        out_specs=(P(("grp", "sp"), None), P("sp", None, None, "grp", None)),
        check_vma=False,
    )
```
